32 devices in a mesh: row: 16 (over z, y, core), col: 2 (over x).
Axes of the slice: x: 2, y: 2, z: 4, core: 2. Of those that a mesh axis runs over, the one named last changes fastest.
Arguments:
- samples: float32 [256, 16384], P(None, 'col'), may hold values from -0.8 to 0.8
- values: float32 [16384, 16384], P('row', 'col'), may hold values from -6 to 6
- diag_entries: float32 [16384], P('row'), may hold values from 16 to 32
- block_mask: int32 [64, 64], replicated, may hold values 0 or 1
Outputs:
- updated: float32 [16384, 16384], P('row', 'col')
The draws below stay inside these ranges and needn't reach their ends.
All inputs are finite; a program needn't handle non-finite values.
Results may differ from the reference program's by a relative error of at most 0.0003.
Values sent between devices are 32-bit elements; how exact they have to be, the bound alone decides.
A program may use at most 192 MiB of HBM per device.

```python
import math
import jax
import jax.numpy as jnp
from jax import lax

P_SIZE = 16384
BLOCKS = 64
SAMPLES = 256


def set_ends(entries, key, low, largest):
    longest = entries.shape.index(max(entries.shape))
    spots = []
    for shift in (0, 1):
        where = [jax.random.randint(jax.random.fold_in(key, axis), (), 0, length) for axis, length in enumerate(entries.shape)]
        where[longest] = (where[longest] + shift) % entries.shape[longest]
        spots.append(tuple(where))
    return entries.at[spots[0]].set(low).at[spots[1]].set(largest)


def spiked(result, key, source, target, parts, factor):
    owner, partner = [(jnp.arange(result.shape[dim]) // (result.shape[dim] // parts)).reshape([-1 if axis == dim else 1 for axis in range(result.ndim)]) for dim in (source, target)]
    chosen = jax.random.permutation(key, parts)[partner]
    strong = (owner == chosen) | (owner == (partner + parts // 2) % parts)
    return jnp.where(strong, factor * result, result)


def steps_of(stream_key, dims, shards, low, high):
    loudness, own = 1.0, jax.random.fold_in(stream_key, 6)
    for axis_at, shards_of in shards:
        heights = jnp.exp(jax.random.uniform(jax.random.fold_in(own, axis_at), (shards_of,), jnp.float32, low / len(shards), high / len(shards)))
        loudness = loudness * jnp.repeat(heights, dims[axis_at] // shards_of).reshape([-1 if axis == axis_at else 1 for axis in range(len(dims))])
    return loudness


def centred(key, extent, spread, most, cuts=(), held_as=jnp.bfloat16):
    values = jax.random.normal(key, extent, jnp.float32) * spread
    if len(cuts) > 0:
        values = steps_of(key, extent, cuts, -0.22, 0.18) * values
    return jnp.clip(values, min=-most, max=most).astype(held_as)


def noise_with(stream_key, shape, spread, reach, pieces, heavy, held_as=jnp.bfloat16):
    values = spread * jax.random.normal(stream_key, shape, jnp.float32)
    if pieces:
        values = values * steps_of(stream_key, shape, pieces, -0.22, 0.18)
    return jnp.clip(spiked(values, jax.random.fold_in(stream_key, 3), *heavy), -reach, reach).astype(held_as)


def setup_inputs(seed: int = 0) -> dict:
    keys = jax.random.split(jax.random.key(seed), 5)
    samples = noise_with(keys[0], (SAMPLES, P_SIZE), 0.13, 0.8, ((1, 2),), (1, 0, 2, 2.0), jnp.float32)
    values = centred(keys[1], (P_SIZE, P_SIZE), 1.0, 6.0, ((0, 16), (1, 2)), jnp.float32)
    diag_entries = jnp.clip(jnp.exp(math.log(32.0) - 0.6931472 * jax.random.uniform(keys[2], (P_SIZE,), jnp.float32) ** steps_of(keys[2], (P_SIZE,), ((0, 16),), -0.2, 0.2)), 16.0, 32.0)
    block_mask = set_ends((jax.random.randint(keys[3], (BLOCKS, BLOCKS), 0, 2) < 1).astype(jnp.int32), jax.random.fold_in(keys[3], 1), 0, 1)
    return dict(samples=samples, values=values, diag_entries=diag_entries, block_mask=block_mask)


step_size = 8.0
penalty = 0.05


def reference(samples, values, diag_entries, block_mask):
    order_total = values.shape[0]
    mask_block = order_total // BLOCKS
    dense_mask = jnp.repeat(jnp.repeat(block_mask, mask_block, axis=0), mask_block, axis=1).astype(jnp.float32)
    indices = jnp.arange(order_total, dtype=jnp.int32)
    on_diag = indices[:, None] == indices[None, :]
    omega = jnp.where(on_diag, diag_entries[:, None], dense_mask * values)
    projected = jnp.dot(samples, omega, precision=lax.Precision.HIGHEST, preferred_element_type=jnp.float32)
    sample_count = samples.shape[0]
    row_block = order_total // BLOCKS

    def update_rows(block_index):
        begin = (block_index * row_block).astype(jnp.int32)
        x_rows = lax.dynamic_slice_in_dim(samples, begin, row_block, 1)
        y_rows = lax.dynamic_slice_in_dim(projected, begin, row_block, 1)
        w_rows = lax.dot_general(x_rows, projected, (((0,), (0,)), ((), ())), precision=lax.Precision.HIGHEST, preferred_element_type=jnp.float32)
        wt_rows = lax.dot_general(y_rows, samples, (((0,), (0,)), ((), ())), precision=lax.Precision.HIGHEST, preferred_element_type=jnp.float32)
        gradient = 0.5 * (w_rows / sample_count + wt_rows / sample_count)
        row_ids = begin + jnp.arange(row_block, dtype=jnp.int32)
        diag_here = row_ids[:, None] == indices[None, :]
        diag_rows = lax.dynamic_slice_in_dim(diag_entries, begin, row_block, 0)
        gradient = gradient - jnp.where(diag_here, 1.0 / diag_rows[:, None], jnp.float32(0.0))
        omega_rows = lax.dynamic_slice_in_dim(omega, begin, row_block, 0)
        stepped = omega_rows - step_size * gradient
        shrunk = jnp.sign(stepped) * jnp.maximum(jnp.abs(stepped) - step_size * penalty, jnp.float32(0.0))
        return jnp.where(diag_here, stepped, shrunk)

    blocks_out = lax.map(update_rows, jnp.arange(BLOCKS, dtype=jnp.int32))
    return blocks_out.reshape(order_total, order_total)
```

```python
import functools

import jax
import jax.numpy as jnp
from jax import lax
from jax.experimental import pallas as pl
from jax.experimental.pallas import tpu as pltpu
from jax.sharding import PartitionSpec as P

step_size = 8.0
penalty = 0.05
MESH = pl.DeviceIdType.MESH
VM = pltpu.VMEM
LIMIT = 60 * 1024 * 1024
SLACK = 2
NEAR = 1


def split(x):
    high = x.astype(jnp.bfloat16)
    low = (x - high.astype(jnp.float32)).astype(jnp.bfloat16)
    return high, low


def dot(a, b):
    return jnp.dot(a, b, preferred_element_type=jnp.float32)


def on_diagonal(row_at, col_at, shape):
    rows = lax.broadcasted_iota(jnp.int32, shape, 0) + row_at
    cols = lax.broadcasted_iota(jnp.int32, shape, 1) + col_at
    return rows == cols


def masked(mask_ref, values, row_at, col_at, block):
    pieces = [
        values[:, at : at + block] * mask_ref[row_at // block, (col_at + at) // block].astype(jnp.float32)
        for at in range(0, values.shape[1], block)
    ]
    return jnp.concatenate(pieces, axis=1)


def crosses(row_at, col_at, shape):
    return jnp.logical_and(row_at < col_at + shape[1], col_at < row_at + shape[0])


def update_kernel(left_ref, proj_ref, samples_ref, values_ref, diag_ref, mask_ref, out_ref, lefts, rights):
    step = pl.program_id(0)
    count = samples_ref.shape[0]
    height, tile = values_ref.shape
    spans, deep = proj_ref.shape[0], proj_ref.shape[2]
    both = 2 * count
    block = lax.axis_size("col") * pl.num_programs(0) * tile // mask_ref.shape[0]
    row_at = lax.axis_index("row") * height
    col_at = (lax.axis_index("col") * pl.num_programs(0) + step) * tile

    @pl.when(step == 0)
    def _():
        high, low = split(left_ref[...].T * (0.5 * step_size / count))
        lefts[:, :both] = high
        lefts[:, both:] = low

    def place(at, value):
        high, low = split(value)
        rights[at : at + value.shape[0], :] = high
        rights[both + at : both + at + value.shape[0], :] = low

    for span in range(spans):
        place(span * deep, proj_ref[span, 0])
    place(count, samples_ref[...])
    limit = step_size * penalty

    def update(hit):
        for begin in range(0, height, block):
            rows = pl.ds(begin, block)
            left_high, left_low = lefts[rows, :both], lefts[rows, both:]
            cross = dot(left_high, rights[:both, :]) + dot(left_low, rights[:both, :]) + dot(left_high, rights[both:, :])
            omega = masked(mask_ref, values_ref[rows, :], row_at + begin, col_at, block)
            stepped = omega - cross
            new = stepped - jnp.clip(stepped, -limit, limit)
            if hit:
                diag = diag_ref[:, pl.ds(pl.multiple_of(col_at - row_at, tile), tile)]
                new = jnp.where(
                    on_diagonal(row_at + begin, col_at, new.shape), diag - cross + step_size / diag, new
                )
            out_ref[rows, :] = new

    hit = crosses(row_at, col_at, (height, tile))
    pl.when(hit)(lambda: update(True))
    pl.when(jnp.logical_not(hit))(lambda: update(False))


def reduce_kernel(
    lines, groups, per_group, samples_ref, values_ref, diag_ref, mask_ref, out_ref, left_ref, *scratch
):
    part, core_in, y_in, a_in, a_mid, b_low, b_high, rung = scratch[:8]
    send, recv, held, lefts, rights, held_sem, fetch_send, fetch_sem, proj_send, proj_sem = scratch[8:]
    row, col = lax.axis_index("row"), lax.axis_index("col")
    core, side, line = row % 2, row // 2 % 2, row // 4
    last, middle = lines - 1, lines // 2
    core_mate = row + 1 - 2 * core
    y_mate = row + 2 - 4 * side
    up, down = row + 4, row - 4
    lower = line < middle
    inner = jnp.where(lower, up, down)
    outer = jnp.where(lower, down, up)
    depth = jnp.where(lower, line, last - line)
    is_mid = depth == middle - 1
    chunks, deep, width = part.shape
    half, piece = deep // 2, deep // 8
    spans = chunks // per_group
    samples = deep * spans
    height = values_ref.shape[0]
    columns = per_group * width
    block = groups * columns // mask_ref.shape[0]
    has_up, has_down = line < last, line > 0
    owner = row // per_group
    mine_at = row % per_group

    barrier = pltpu.get_barrier_semaphore()

    def greet(target):
        pl.semaphore_signal(barrier, inc=1, device_id=target, device_id_type=MESH)

    def load(i):
        slot = i % 2
        at = pl.multiple_of(i % per_group * width, width)
        return pltpu.make_async_copy(values_ref.at[:, pl.ds(at, width)], held.at[slot], held_sem.at[slot])

    load(0).start()
    load(1).start()
    greet((core_mate, col))
    greet((y_mate, col))
    pl.when(has_up)(lambda: greet((up, col)))
    pl.when(has_down)(lambda: greet((down, col)))
    for shift in range(1, groups):
        greet((row, lax.rem(col + shift, groups)))
    ends = jnp.where(has_up, 1, 0) + jnp.where(has_down, 1, 0)
    pl.semaphore_wait(barrier, 2 + groups - 1 + ends)

    def rows_at(at, size):
        return pl.ds(pl.multiple_of(at, piece), size)

    def copy(kind, q, source, target, device, landing=None):
        return pltpu.make_async_remote_copy(
            src_ref=source,
            dst_ref=target,
            send_sem=send.at[kind, q],
            recv_sem=recv.at[kind if landing is None else landing, q],
            device_id=(device, col),
            device_id_type=MESH,
        )

    def spread(kind, q, at, size, device, landing=None):
        rows = out_ref.at[q, rows_at(at, size), :]
        return copy(kind, q, rows, rows, device, landing)

    own_half = core * half
    b_own = [flow * piece for flow in range(2)]
    roots = [middle - 1, middle]
    a_own = 2 * piece + side * piece
    a_other = 2 * piece + (1 - side) * piece

    def c_core(q):
        return copy(0, q, part.at[q, rows_at((1 - core) * half, half), :], core_in.at[q], core_mate)

    def c_y(q):
        return copy(1, q, core_in.at[q, rows_at(a_other, piece), :], y_in.at[q], y_mate)

    def c_a_in(q):
        return copy(2, q, y_in.at[q], a_in.at[q], inner)

    def c_a_mid(q):
        return copy(3, q, y_in.at[q], a_mid.at[q], inner)

    def c_a_out(q):
        return spread(4, q, own_half + a_own, piece, outer)

    def c_y_back(q):
        return spread(5, q, own_half + a_own, piece, y_mate)

    def y_back_arrival(q):
        return spread(5, q, own_half + a_other, piece, y_mate)

    def c_b_up(q, flow):
        return copy(6 + flow, q, core_in.at[q, rows_at(b_own[flow], piece), :], b_low.at[flow, q], up)

    def c_b_down(q, flow):
        return copy(8 + flow, q, core_in.at[q, rows_at(b_own[flow], piece), :], b_high.at[flow, q], down)

    def c_rung(q, flow):
        return copy(10, q, core_in.at[q, rows_at(b_own[flow], piece), :], rung.at[q], y_mate)

    def c_b_out(q, flow, upward):
        return spread(11 + 2 * flow + upward, q, own_half + b_own[flow], piece, up if upward else down, 11 + flow)

    def c_core_back(q):
        return spread(15, q, own_half, half, core_mate)

    def core_arrival(q):
        return spread(15, q, half - own_half, half, core_mate)

    def at_stage(t, offset, condition, action):
        q = t - offset
        live = jnp.logical_and(q >= 0, q < chunks)
        if condition is not None:
            live = jnp.logical_and(live, condition)
        pl.when(live)(lambda: action(jnp.clip(q, 0, chunks - 1)))

    def b_rows(flow):
        return pl.ds(b_own[flow], piece)

    def a_forward(q):
        pl.when(is_mid)(lambda: c_a_mid(q).start())
        pl.when(jnp.logical_not(is_mid))(lambda: c_a_in(q).start())

    def begin(q):
        c_core(q).wait_recv()
        core_in[q] = core_in[q] + part[q, rows_at(own_half, half), :]
        c_y(q).start()
        for flow in range(2):
            if roots[flow] > 0:
                pl.when(line == 0)(lambda flow=flow: c_b_up(q, flow).start())
            if roots[flow] < last:
                pl.when(line == last)(lambda flow=flow: c_b_down(q, flow).start())

    def after_y(q):
        c_y(q).wait_recv()
        y_in[q] = y_in[q] + core_in[q, rows_at(a_own, piece), :]
        pl.when(depth == 0)(lambda: a_forward(q))

    def a_reduce(q):
        c_a_in(q).wait_recv()
        y_in[q] = y_in[q] + a_in[q]
        a_forward(q)

    def a_total(q):
        c_a_mid(q).wait_recv()
        out_ref[q, rows_at(own_half + a_own, piece), :] = y_in[q] + a_mid[q]
        pl.when(depth > 0)(lambda: c_a_out(q).start())
        c_y_back(q).start()

    def a_back(q):
        c_a_out(q).wait_recv()
        pl.when(depth > 0)(lambda: c_a_out(q).start())
        c_y_back(q).start()

    def b_pass_up(q, flow):
        c_b_up(q, flow).wait_recv()
        core_in[q, b_rows(flow), :] = core_in[q, b_rows(flow), :] + b_low[flow, q]
        c_b_up(q, flow).start()

    def b_pass_down(q, flow):
        c_b_down(q, flow).wait_recv()
        core_in[q, b_rows(flow), :] = core_in[q, b_rows(flow), :] + b_high[flow, q]
        c_b_down(q, flow).start()

    def b_root(q, flow):
        if roots[flow] > 0:
            c_b_up(q, flow).wait_recv()
            core_in[q, b_rows(flow), :] = core_in[q, b_rows(flow), :] + b_low[flow, q]
        if roots[flow] < last:
            c_b_down(q, flow).wait_recv()
            core_in[q, b_rows(flow), :] = core_in[q, b_rows(flow), :] + b_high[flow, q]
        c_rung(q, flow).start()

    def b_total(q, flow):
        c_rung(q, flow).wait_recv()
        out_ref[q, rows_at(own_half + b_own[flow], piece), :] = core_in[q, b_rows(flow), :] + rung[q]
        if roots[flow] > 0:
            c_b_out(q, flow, 0).start()
        if roots[flow] < last:
            c_b_out(q, flow, 1).start()

    def b_back(q, flow):
        c_b_out(q, flow, 0).wait_recv()
        pl.when(jnp.logical_and(line < roots[flow], has_down))(lambda: c_b_out(q, flow, 0).start())
        pl.when(jnp.logical_and(line > roots[flow], has_up))(lambda: c_b_out(q, flow, 1).start())

    def gather(q):
        y_back_arrival(q).wait_recv()
        c_core_back(q).start()

    def slice_rows(q):
        return pl.ds(pl.multiple_of(q // per_group * deep, deep), deep)

    def c_proj(q, shift):
        span = q // per_group
        return pltpu.make_async_remote_copy(
            src_ref=out_ref.at[q],
            dst_ref=left_ref.at[pl.ds(pl.multiple_of(samples + span * deep, deep), deep), :],
            send_sem=proj_send.at[shift, span],
            recv_sem=proj_sem.at[span],
            device_id=(row, lax.rem(col + shift, groups)),
            device_id_type=MESH,
        )

    is_owner = col == owner

    def finish(q):
        core_arrival(q).wait_recv()

        @pl.when(jnp.logical_and(is_owner, q % per_group == mine_at))
        def _():
            for shift in range(1, groups):
                c_proj(q, shift).start()
            left_ref[pl.ds(pl.multiple_of(samples + q // per_group * deep, deep), deep), :] = out_ref[q]

    slice_at = pl.multiple_of(mine_at * width, width)

    def fetched(span):
        rows = pl.ds(span * deep, deep)
        return samples_ref.at[rows, pl.ds(slice_at, width)], left_ref.at[rows, :]

    def fetch(shift, span):
        source, target = fetched(span)
        return pltpu.make_async_remote_copy(
            src_ref=source,
            dst_ref=target,
            send_sem=fetch_send.at[shift, span],
            recv_sem=fetch_sem.at[0, span],
            device_id=(row, lax.rem(col + shift, groups)),
            device_id_type=MESH,
        )

    def own(span):
        return pltpu.make_async_copy(*fetched(span), fetch_sem.at[1, span])

    @pl.when(is_owner)
    def _():
        for span in range(spans):
            for shift in range(1, groups):
                fetch(shift, span).start()
            own(span).start()

    def take(first, count):
        @pl.when(is_owner)
        def _():
            for span in range(first, first + count):
                own(span).wait()

        @pl.when(jnp.logical_not(is_owner))
        def _():
            for span in range(first, first + count):
                fetch(1, span).wait_recv()

        size = count * deep
        high, low = split(left_ref[pl.ds(first * deep, size), :])
        lefts[2 * first * deep : 2 * first * deep + size, :] = high
        lefts[2 * first * deep + size : 2 * (first * deep + size), :] = low

    def project(i, first, count):
        load(i).wait()
        slot = i % 2
        span_at = i % per_group
        hit = jnp.logical_and(is_owner, span_at == mine_at)
        size = count * deep
        base = 2 * first * deep

        @pl.loop(0, width // block)
        def _(b):
            cols = pl.ds(pl.multiple_of(b * block, block), block)
            mask_col = (col * columns + span_at * width) // block + b

            def put(rows, omega):
                high, low = split(omega)
                rights[0, rows, :] = high
                rights[1, rows, :] = low

            def omega_at(k):
                rows = pl.ds(pl.multiple_of(k * block, block), block)
                return held[slot, rows, cols] * mask_ref[row * height // block + k, mask_col].astype(jnp.float32)

            for k in range(height // block):
                put(pl.ds(k * block, block), omega_at(k))

            @pl.when(hit)
            def _():
                omega = omega_at(b)
                omega = jnp.where(on_diagonal(0, 0, omega.shape), diag_ref[:, cols], omega)
                put(cols, omega)

            both = dot(lefts[base : base + 2 * size, :], rights[0])
            total = both[:size, :] + both[size:, :] + dot(lefts[base : base + size, :], rights[1])
            for s in range(count):
                part[(first + s) * per_group + span_at, :, cols] = total[s * deep : (s + 1) * deep, :]

        pl.when(i + 2 < 2 * per_group)(lambda: load(i + 2).start())

    take(0, 1)
    slack = SLACK
    near = NEAR

    @pl.loop(0, chunks + 2 * near + slack * (lines + 1) + 1)
    def _(t):
        pl.when(t < per_group)(lambda: project(t, 0, 1))
        pl.when(t == per_group)(lambda: take(1, spans - 1))
        pl.when(jnp.logical_and(t >= per_group, t < 2 * per_group))(lambda: project(t, 1, spans - 1))
        at_stage(t, 0, None, lambda q: c_core(q).start())
        at_stage(t, near, None, begin)
        t = t - near
        at_stage(t, slack, None, after_y)
        for flow in range(2):
            root = roots[flow]
            if root > 1:
                at_stage(t, slack * line, jnp.logical_and(line > 0, line < root), lambda q, flow=flow: b_pass_up(q, flow))
            if root < last - 1:
                at_stage(t, slack * (last - line), jnp.logical_and(line > root, line < last), lambda q, flow=flow: b_pass_down(q, flow))
        if middle > 1:
            at_stage(t, slack * (1 + depth), depth > 0, a_reduce)
        for flow in range(2):
            at_stage(t, slack * middle, line == roots[flow], lambda q, flow=flow: b_root(q, flow))
        at_stage(t, slack * (1 + middle), is_mid, a_total)
        for flow in range(2):
            at_stage(t, slack * (1 + middle), line == roots[flow], lambda q, flow=flow: b_total(q, flow))
        if middle > 1:
            at_stage(t, slack * (lines - depth), jnp.logical_not(is_mid), a_back)
        for flow in range(2):
            away = jnp.abs(line - roots[flow])
            at_stage(t, slack * (1 + middle + away), away > 0, lambda q, flow=flow: b_back(q, flow))
        at_stage(t, slack * (lines + 1 - depth), None, gather)
        at_stage(t, near + slack * (lines + 1 - depth), None, finish)

    @pl.loop(0, chunks)
    def _(q):
        c_core(q).wait_send()
        c_y(q).wait_send()
        pl.when(is_mid)(lambda: c_a_mid(q).wait_send())
        pl.when(jnp.logical_not(is_mid))(lambda: c_a_in(q).wait_send())
        pl.when(depth > 0)(lambda: c_a_out(q).wait_send())
        c_y_back(q).wait_send()
        for flow in range(2):
            root = roots[flow]
            pl.when(line < root)(lambda flow=flow: c_b_up(q, flow).wait_send())
            pl.when(line > root)(lambda flow=flow: c_b_down(q, flow).wait_send())
            pl.when(line == root)(lambda flow=flow: c_rung(q, flow).wait_send())
            pl.when(jnp.logical_and(line <= root, has_down))(lambda flow=flow: c_b_out(q, flow, 0).wait_send())
            pl.when(jnp.logical_and(line >= root, has_up))(lambda flow=flow: c_b_out(q, flow, 1).wait_send())
        c_core_back(q).wait_send()

    @pl.when(is_owner)
    def _():
        for span in range(spans):
            for shift in range(1, groups):
                fetch(shift, span).wait_send()
                c_proj(span * per_group, shift).wait_send()

    @pl.when(jnp.logical_not(is_owner))
    def _():
        for span in range(spans):
            c_proj(span * per_group, 1).wait_recv()


def per_device(samples, values, diag_entries, block_mask):
    height, order = values.shape
    count = samples.shape[0]
    groups = lax.axis_size("col")
    lines = lax.axis_size("row") // 4
    per_group = order // height
    block = groups * order // block_mask.shape[0]
    diag = diag_entries[None, :]
    anywhere = pl.BlockSpec(memory_space=pl.ANY)
    in_smem = pl.BlockSpec(memory_space=pltpu.SMEM)
    in_vmem = pl.BlockSpec(memory_space=VM)
    deep = min(64, count // 2)
    spans = count // deep
    chunks = spans * per_group
    piece = deep // 8
    kinds = 16
    flows = lambda *lead: VM((*lead, chunks, piece, height), jnp.float32)
    dma = pltpu.SemaphoreType.DMA
    projected, left = pl.pallas_call(
        functools.partial(reduce_kernel, lines, groups, per_group),
        out_shape=(
            jax.ShapeDtypeStruct((chunks, deep, height), jnp.float32),
            jax.ShapeDtypeStruct((2 * count, height), jnp.float32),
        ),
        in_specs=[anywhere, anywhere, in_vmem, in_smem],
        out_specs=(in_vmem, in_vmem),
        scratch_shapes=[
            VM((chunks, deep, height), jnp.float32),
            VM((chunks, deep // 2, height), jnp.float32),
            flows(),
            flows(),
            flows(),
            flows(2),
            flows(2),
            flows(),
            dma((kinds, chunks)),
            dma((kinds, chunks)),
            VM((2, height, height), jnp.float32),
            VM((2 * count, height), jnp.bfloat16),
            VM((2, height, block), jnp.bfloat16),
            dma((2,)),
            dma((groups, spans)),
            dma((2, spans)),
            dma((groups, spans)),
            dma((spans,)),
        ],
        compiler_params=pltpu.CompilerParams(
            collective_id=1, has_side_effects=True, vmem_limit_bytes=LIMIT
        ),
    )(samples, values, diag, block_mask)

    tile = height
    grid = order // tile
    fixed = lambda shape: pl.BlockSpec(shape, lambda i: (0, 0))
    moving = lambda rows: pl.BlockSpec((rows, tile), lambda i: (0, i))
    return pl.pallas_call(
        update_kernel,
        out_shape=jax.ShapeDtypeStruct((height, order), jnp.float32),
        grid=(grid,),
        in_specs=[
            fixed((2 * count, height)),
            pl.BlockSpec((spans, 1, deep, tile), lambda i: (0, i, 0, 0)),
            moving(count),
            moving(height),
            fixed((1, height)),
            in_smem,
        ],
        out_specs=moving(height),
        scratch_shapes=[
            VM((height, 4 * count), jnp.bfloat16),
            VM((4 * count, tile), jnp.bfloat16),
        ],
        compiler_params=pltpu.CompilerParams(dimension_semantics=("arbitrary",), vmem_limit_bytes=LIMIT),
    )(left, projected.reshape(spans, per_group, deep, height), samples, values, diag, block_mask)


def solution(mesh):
    in_specs = (P(None, "col"), P("row", "col"), P("row"), P())
    out_specs = P("row", "col")
    return jax.shard_map(
        per_device, mesh=mesh, in_specs=in_specs, out_specs=out_specs, check_vma=False
    )
```

```python
import functools

import jax
import jax.numpy as jnp
from jax import lax
from jax.experimental import pallas as pl
from jax.experimental.pallas import tpu as pltpu
from jax.sharding import PartitionSpec as P

step_size = 8.0
penalty = 0.05
MESH = pl.DeviceIdType.MESH
VM = pltpu.VMEM
REDUCE_LIMIT = 21 * 1024 * 1024
UPDATE_LIMIT = 14 * 1024 * 1024
SLACK = 2
NEAR = 1
PARTS = 1
EARLY_WAIT = 0


def split(x):
    high = x.astype(jnp.bfloat16)
    low = (x - high.astype(jnp.float32)).astype(jnp.bfloat16)
    return high, low


def dot(a, b):
    return jnp.dot(a, b, preferred_element_type=jnp.float32)


def on_diagonal(row_at, col_at, shape):
    rows = lax.broadcasted_iota(jnp.int32, shape, 0) + row_at
    cols = lax.broadcasted_iota(jnp.int32, shape, 1) + col_at
    return rows == cols


def masked(mask_ref, values, row_at, col_at, block):
    pieces = [
        values[:, at : at + block] * mask_ref[row_at // block, (col_at + at) // block].astype(jnp.float32)
        for at in range(0, values.shape[1], block)
    ]
    return jnp.concatenate(pieces, axis=1)


def crosses(row_at, col_at, shape):
    return jnp.logical_and(row_at < col_at + shape[1], col_at < row_at + shape[0])


def fill_lefts(lefts, left_ref, first, size):
    count = left_ref.shape[0] // 2
    for at, source in ((0, first), (size, count + first)):
        high, low = split(left_ref[source : source + size, :].T * (0.5 * step_size / count))
        lefts[:, at : at + size] = high
        lefts[:, 2 * size + at : 3 * size + at] = low
        lefts[:, 4 * size + at : 5 * size + at] = high


def fill_rights(rights, at, value):
    both = rights.shape[0] // 3
    high, low = split(value)
    rights[at : at + value.shape[0], :] = high
    rights[both + at : both + at + value.shape[0], :] = high
    rights[2 * both + at : 2 * both + at + value.shape[0], :] = low


def cross_of(lefts, rights, rows):
    return dot(lefts[rows, :], rights[...])


def update_kernel(
    first, per_group, left_ref, held_ref, samples_ref, diag_ref, out_ref,
    lefts, rights, sample_tiles, out_tiles, sample_sem, out_sem,
):
    height, tile = out_tiles.shape[1:]
    size = sample_tiles.shape[1]
    columns = held_ref.shape[1]
    width = columns // per_group
    steps = columns // tile
    proj_at = height + first
    row_at = lax.axis_index("row") * height
    col_base = lax.axis_index("col") * per_group * width
    block = height
    limit = step_size * penalty

    def columns_at(u):
        return pl.ds(pl.multiple_of(u * tile, tile), tile)

    def load(u):
        source = samples_ref.at[pl.ds(first, size), columns_at(u)]
        return pltpu.make_async_copy(source, sample_tiles.at[u % 2], sample_sem.at[u % 2])

    def store(u):
        return pltpu.make_async_copy(out_tiles.at[u % 2], out_ref.at[:, columns_at(u)], out_sem.at[u % 2])

    load(0).start()
    load(1).start()
    fill_lefts(lefts, left_ref, first, size)

    @pl.loop(0, steps)
    def _(u):
        slot = u % 2
        load(u).wait()
        fill_rights(rights, 0, held_ref[proj_at : proj_at + size, columns_at(u)])
        fill_rights(rights, size, sample_tiles[slot])
        pl.when(u + 2 < steps)(lambda: load(u + 2).start())
        pl.when(u >= 2)(lambda: store(u - 2).wait())
        col_at = col_base + u * tile

        def update(hit):
            for begin in range(0, height, block):
                rows = pl.ds(begin, block)
                stepped = held_ref[rows, columns_at(u)] - cross_of(lefts, rights, rows)
                new = stepped - jnp.clip(stepped, -limit, limit)
                if hit:
                    diag = diag_ref[:, pl.ds(pl.multiple_of(col_at - row_at, tile), tile)]
                    new = jnp.where(on_diagonal(row_at + begin, col_at, new.shape), stepped + step_size / diag, new)
                out_tiles[slot, rows, :] = new

        hit = crosses(row_at, col_at, (height, tile))
        pl.when(hit)(lambda: update(True))
        pl.when(jnp.logical_not(hit))(lambda: update(False))
        store(u).start()

    for u in range(max(0, steps - 2), steps):
        store(u).wait()


def reduce_kernel(
    lines, groups, per_group, early, samples_ref, values_ref, diag_ref, mask_ref, left_ref, held, *scratch
):
    core_in, y_in, a_in, a_mid, b_low, b_high, rung = scratch[:7]
    send, core_send, recv, lefts, rights, held_sem, fetch_send, fetch_sem, proj_send, proj_sem = scratch[7:17]
    early_lefts, early_rights, sample_tiles, sample_sem = scratch[17:]
    row, col = lax.axis_index("row"), lax.axis_index("col")
    core, side, line = row % 2, row // 2 % 2, row // 4
    last, middle = lines - 1, lines // 2
    core_mate = row + 1 - 2 * core
    y_mate = row + 2 - 4 * side
    up, down = row + 4, row - 4
    lower = line < middle
    inner = jnp.where(lower, up, down)
    outer = jnp.where(lower, down, up)
    depth = jnp.where(lower, line, last - line)
    is_mid = depth == middle - 1
    height, columns = values_ref.shape
    width = columns // per_group
    chunks, half, wide = core_in.shape
    deep, piece = 2 * half, half // 4
    parts = width // wide
    per_span = per_group * parts
    spans = chunks // per_span
    samples = deep * spans
    block = groups * columns // mask_ref.shape[0]
    has_up, has_down = line < last, line > 0
    owner = row // per_group
    mine_at = row % per_group

    barrier = pltpu.get_barrier_semaphore()

    def greet(target):
        pl.semaphore_signal(barrier, inc=1, device_id=target, device_id_type=MESH)

    def load(i):
        cols = pl.ds(pl.multiple_of(i * width, width), width)
        return pltpu.make_async_copy(values_ref.at[:, cols], held.at[pl.ds(0, height), cols], held_sem.at[i])

    for i in range(2):
        load(i).start()
    greet((core_mate, col))
    greet((y_mate, col))
    pl.when(has_up)(lambda: greet((up, col)))
    pl.when(has_down)(lambda: greet((down, col)))
    for shift in range(1, groups):
        greet((row, lax.rem(col + shift, groups)))
    ends = jnp.where(has_up, 1, 0) + jnp.where(has_down, 1, 0)
    pl.semaphore_wait(barrier, 2 + groups - 1 + ends)

    def rows_at(at, size):
        return pl.ds(pl.multiple_of(at, piece), size)

    def copy(kind, q, source, target, device, landing=None):
        return pltpu.make_async_remote_copy(
            src_ref=source,
            dst_ref=target,
            send_sem=send.at[kind] if kind else core_send.at[q],
            recv_sem=recv.at[kind if landing is None else landing, q],
            device_id=(device, col),
            device_id_type=MESH,
        )

    def place(q, at, size):
        return (
            rows_at(height + q // per_span * deep + at, size),
            pl.ds(pl.multiple_of(q % per_span * wide, wide), wide),
        )

    def spread(kind, q, at, size, device, landing=None):
        rows = held.at[place(q, at, size)]
        return copy(kind, q, rows, rows, device, landing)

    own_half = core * half
    b_own = [flow * piece for flow in range(2)]
    roots = [middle - 1, middle]
    a_own = 2 * piece + side * piece
    a_other = 2 * piece + (1 - side) * piece

    def c_core(q):
        return copy(0, q, held.at[place(q, (1 - core) * half, half)], core_in.at[q], core_mate)

    def c_y(q):
        return copy(1, q, core_in.at[q, rows_at(a_other, piece), :], y_in.at[q], y_mate)

    def c_a_in(q):
        return copy(2, q, y_in.at[q], a_in.at[q], inner)

    def c_a_mid(q):
        return copy(3, q, y_in.at[q], a_mid.at[q], inner)

    def c_a_out(q):
        return spread(4, q, own_half + a_own, piece, outer)

    def c_y_back(q):
        return spread(5, q, own_half + a_own, piece, y_mate)

    def y_back_arrival(q):
        return spread(5, q, own_half + a_other, piece, y_mate)

    def c_b_up(q, flow):
        return copy(6 + flow, q, core_in.at[q, rows_at(b_own[flow], piece), :], b_low.at[flow, q], up)

    def c_b_down(q, flow):
        return copy(8 + flow, q, core_in.at[q, rows_at(b_own[flow], piece), :], b_high.at[flow, q], down)

    def c_rung(q, flow):
        return copy(10, q, core_in.at[q, rows_at(b_own[flow], piece), :], rung.at[q], y_mate)

    def c_b_out(q, flow, upward):
        return spread(11 + 2 * flow + upward, q, own_half + b_own[flow], piece, up if upward else down, 11 + flow)

    def c_core_back(q):
        return spread(15, q, own_half, half, core_mate)

    def core_arrival(q):
        return spread(15, q, half - own_half, half, core_mate)

    def at_stage(t, offset, condition, action):
        q = t - offset
        live = jnp.logical_and(q >= 0, q < chunks)
        if condition is not None:
            live = jnp.logical_and(live, condition)
        pl.when(live)(lambda: action(jnp.clip(q, 0, chunks - 1)))

    def b_rows(flow):
        return pl.ds(b_own[flow], piece)

    def a_forward(q):
        pl.when(is_mid)(lambda: c_a_mid(q).start())
        pl.when(jnp.logical_not(is_mid))(lambda: c_a_in(q).start())

    def begin(q):
        c_core(q).wait()
        core_in[q] = core_in[q] + held[place(q, own_half, half)]
        c_y(q).start()
        for flow in range(2):
            if roots[flow] > 0:
                pl.when(line == 0)(lambda flow=flow: c_b_up(q, flow).start())
            if roots[flow] < last:
                pl.when(line == last)(lambda flow=flow: c_b_down(q, flow).start())

    def after_y(q):
        c_y(q).wait_recv()
        y_in[q] = y_in[q] + core_in[q, rows_at(a_own, piece), :]
        pl.when(depth == 0)(lambda: a_forward(q))

    def a_reduce(q):
        c_a_in(q).wait_recv()
        y_in[q] = y_in[q] + a_in[q]
        a_forward(q)

    def a_total(q):
        c_a_mid(q).wait_recv()
        held[place(q, own_half + a_own, piece)] = y_in[q] + a_mid[q]
        pl.when(depth > 0)(lambda: c_a_out(q).start())
        c_y_back(q).start()

    def a_back(q):
        c_a_out(q).wait_recv()
        pl.when(depth > 0)(lambda: c_a_out(q).start())
        c_y_back(q).start()

    def b_pass_up(q, flow):
        c_b_up(q, flow).wait_recv()
        core_in[q, b_rows(flow), :] = core_in[q, b_rows(flow), :] + b_low[flow, q]
        c_b_up(q, flow).start()

    def b_pass_down(q, flow):
        c_b_down(q, flow).wait_recv()
        core_in[q, b_rows(flow), :] = core_in[q, b_rows(flow), :] + b_high[flow, q]
        c_b_down(q, flow).start()

    def b_root(q, flow):
        if roots[flow] > 0:
            c_b_up(q, flow).wait_recv()
            core_in[q, b_rows(flow), :] = core_in[q, b_rows(flow), :] + b_low[flow, q]
        if roots[flow] < last:
            c_b_down(q, flow).wait_recv()
            core_in[q, b_rows(flow), :] = core_in[q, b_rows(flow), :] + b_high[flow, q]
        c_rung(q, flow).start()

    def b_total(q, flow):
        c_rung(q, flow).wait_recv()
        held[place(q, own_half + b_own[flow], piece)] = core_in[q, b_rows(flow), :] + rung[q]
        if roots[flow] > 0:
            c_b_out(q, flow, 0).start()
        if roots[flow] < last:
            c_b_out(q, flow, 1).start()

    def b_back(q, flow):
        c_b_out(q, flow, 0).wait_recv()
        pl.when(jnp.logical_and(line < roots[flow], has_down))(lambda: c_b_out(q, flow, 0).start())
        pl.when(jnp.logical_and(line > roots[flow], has_up))(lambda: c_b_out(q, flow, 1).start())

    def gather(q):
        y_back_arrival(q).wait_recv()
        c_core_back(q).start()

    def proj_place(q):
        return (
            pl.ds(pl.multiple_of(samples + q // per_span * deep, deep), deep),
            pl.ds(pl.multiple_of(q % parts * wide, wide), wide),
        )

    def c_proj(q, shift):
        index = q // per_span * parts + q % parts
        return pltpu.make_async_remote_copy(
            src_ref=held.at[place(q, 0, deep)],
            dst_ref=left_ref.at[proj_place(q)],
            send_sem=proj_send.at[shift, index],
            recv_sem=proj_sem.at[index],
            device_id=(row, lax.rem(col + shift, groups)),
            device_id_type=MESH,
        )

    is_owner = col == owner

    def finish(q):
        core_arrival(q).wait_recv()

        @pl.when(jnp.logical_and(is_owner, q % per_span // parts == mine_at))
        def _():
            for shift in range(1, groups):
                c_proj(q, shift).start()
            left_ref[proj_place(q)] = held[place(q, 0, deep)]

    slice_at = pl.multiple_of(mine_at * width, width)

    def fetched(span):
        rows = pl.ds(span * deep, deep)
        return samples_ref.at[rows, pl.ds(slice_at, width)], left_ref.at[rows, :]

    def fetch(shift, span):
        source, target = fetched(span)
        return pltpu.make_async_remote_copy(
            src_ref=source,
            dst_ref=target,
            send_sem=fetch_send.at[shift, span],
            recv_sem=fetch_sem.at[0, span],
            device_id=(row, lax.rem(col + shift, groups)),
            device_id_type=MESH,
        )

    def own(span):
        return pltpu.make_async_copy(*fetched(span), fetch_sem.at[1, span])

    @pl.when(is_owner)
    def _():
        for span in range(spans):
            for shift in range(1, groups):
                fetch(shift, span).start()
            own(span).start()

    def take(first, count):
        @pl.when(is_owner)
        def _():
            for span in range(first, first + count):
                own(span).wait()

        @pl.when(jnp.logical_not(is_owner))
        def _():
            for span in range(first, first + count):
                fetch(1, span).wait_recv()

        size = count * deep
        high, low = split(left_ref[pl.ds(first * deep, size), :])
        lefts[2 * first * deep : 2 * first * deep + size, :] = high
        lefts[2 * first * deep + size : 2 * (first * deep + size), :] = low

    def project(span_at, first, count):
        if first == 0:
            load(span_at).wait()
            pl.when(span_at + 2 < per_group)(lambda: load(span_at + 2).start())
        hit = jnp.logical_and(is_owner, span_at == mine_at)
        size = count * deep
        base = 2 * first * deep

        def put(k, b, omega):
            high, low = split(omega)
            rows, cols = pl.ds(k * block, block), pl.ds(b * block, block)
            rights[0, rows, cols] = high
            rights[1, rows, cols] = low

        def omega_at(k, b):
            cols = pl.ds(pl.multiple_of(span_at * width + b * block, block), block)
            mask_col = (col * columns + span_at * width) // block + b
            keep = mask_ref[row * height // block + k, mask_col].astype(jnp.float32)
            return held[k * block : (k + 1) * block, cols] * keep

        for b in range(width // block):
            for k in range(height // block):
                put(k, b, omega_at(k, b))

        @pl.when(hit)
        def _():
            for b in range(width // block):
                omega = omega_at(b, b)
                diag = diag_ref[:, b * block : (b + 1) * block]
                put(b, b, jnp.where(on_diagonal(0, 0, omega.shape), diag, omega))

        both = dot(lefts[base : base + 2 * size, :], rights[0])
        total = both[:size, :] + both[size:, :] + dot(lefts[base : base + size, :], rights[1])
        cols = pl.ds(pl.multiple_of(span_at * width, width), width)
        held[height + first * deep : height + first * deep + size, cols] = total

    tile = sample_tiles.shape[2]
    steps = columns // tile
    early_size = early * deep
    row_at = row * height

    def load_samples(u):
        cols = pl.ds(pl.multiple_of(u * tile, tile), tile)
        return pltpu.make_async_copy(
            samples_ref.at[pl.ds(0, early_size), cols], sample_tiles.at[u % 2], sample_sem.at[u % 2]
        )

    def arriving(first, end):
        return [span * per_span + part for span in range(first, end) for part in range(parts)]

    def prepare():
        @pl.when(jnp.logical_not(is_owner))
        def _():
            for q in arriving(0, early):
                c_proj(q, 1).wait_recv()

        fill_lefts(early_lefts, left_ref, 0, early_size)

    def step_early(u):
        cols = pl.ds(pl.multiple_of(u * tile, tile), tile)
        load_samples(u).wait()
        fill_rights(early_rights, 0, held[height : height + early_size, cols])
        fill_rights(early_rights, early_size, sample_tiles[u % 2])
        pl.when(u + 2 < steps)(lambda: load_samples(u + 2).start())
        col_at = col * columns + u * tile

        def update(hit):
            for begin_at in range(0, height, block):
                rows = pl.ds(begin_at, block)
                omega = masked(mask_ref, held[rows, cols], row_at + begin_at, col_at, block)
                if hit:
                    diag = diag_ref[:, pl.ds(pl.multiple_of(col_at - row_at, tile), tile)]
                    omega = jnp.where(on_diagonal(row_at + begin_at, col_at, omega.shape), diag, omega)
                held[rows, cols] = omega - cross_of(early_lefts, early_rights, rows)

        hit = crosses(row_at, col_at, (height, tile))
        pl.when(hit)(lambda: update(True))
        pl.when(jnp.logical_not(hit))(lambda: update(False))

    load_samples(0).start()
    load_samples(1).start()
    take(0, 1)
    slack = SLACK
    near = NEAR

    depth_of_pipe = 2 * near + slack * (lines + 1)
    early_at = early * per_span + depth_of_pipe + slack + EARLY_WAIT

    @pl.loop(0, max(chunks + depth_of_pipe, early_at + steps))
    def _(t):
        begin_t = t
        fresh = t % parts == 0
        pl.when(jnp.logical_and(fresh, t < per_span))(lambda: project(t // parts, 0, 1))
        pl.when(t == per_span)(lambda: take(1, spans - 1))
        again = jnp.logical_and(t >= per_span, t < 2 * per_span)
        pl.when(jnp.logical_and(fresh, again))(lambda: project((t - per_span) // parts, 1, spans - 1))
        at_stage(t, 0, None, lambda q: c_core(q).start())
        at_stage(t, near, None, begin)
        t = t - near
        at_stage(t, slack, None, after_y)
        for flow in range(2):
            root = roots[flow]
            if root > 1:
                at_stage(t, slack * line, jnp.logical_and(line > 0, line < root), lambda q, flow=flow: b_pass_up(q, flow))
            if root < last - 1:
                at_stage(t, slack * (last - line), jnp.logical_and(line > root, line < last), lambda q, flow=flow: b_pass_down(q, flow))
        if middle > 1:
            at_stage(t, slack * (1 + depth), depth > 0, a_reduce)
        for flow in range(2):
            at_stage(t, slack * middle, line == roots[flow], lambda q, flow=flow: b_root(q, flow))
        at_stage(t, slack * (1 + middle), is_mid, a_total)
        for flow in range(2):
            at_stage(t, slack * (1 + middle), line == roots[flow], lambda q, flow=flow: b_total(q, flow))
        if middle > 1:
            at_stage(t, slack * (lines - depth), jnp.logical_not(is_mid), a_back)
        for flow in range(2):
            away = jnp.abs(line - roots[flow])
            at_stage(t, slack * (1 + middle + away), away > 0, lambda q, flow=flow: b_back(q, flow))
        at_stage(t, slack * (lines + 1 - depth), None, gather)
        at_stage(t, near + slack * (lines + 1 - depth), None, finish)
        pl.when(begin_t == early_at)(prepare)
        now = begin_t - early_at
        pl.when(jnp.logical_and(now >= 0, now < steps))(lambda: step_early(now))

    def all_sent(kind, ref):
        copy(kind, 0, ref, ref, core_mate).wait_send()

    all_sent(1, y_in)
    pl.when(is_mid)(lambda: all_sent(3, y_in))
    pl.when(jnp.logical_not(is_mid))(lambda: all_sent(2, y_in))
    pl.when(depth > 0)(lambda: all_sent(4, y_in))
    all_sent(5, y_in)
    for flow in range(2):
        root = roots[flow]
        pl.when(line < root)(lambda flow=flow: all_sent(6 + flow, y_in))
        pl.when(line > root)(lambda flow=flow: all_sent(8 + flow, y_in))
        pl.when(line == root)(lambda: all_sent(10, y_in))
        pl.when(jnp.logical_and(line <= root, has_down))(lambda flow=flow: all_sent(11 + 2 * flow, y_in))
        pl.when(jnp.logical_and(line >= root, has_up))(lambda flow=flow: all_sent(12 + 2 * flow, y_in))
    all_sent(15, core_in)

    @pl.when(is_owner)
    def _():
        for span in range(spans):
            for shift in range(1, groups):
                fetch(shift, span).wait_send()
        for q in arriving(0, spans):
            for shift in range(1, groups):
                c_proj(q, shift).wait_send()

    @pl.when(jnp.logical_not(is_owner))
    def _():
        for q in arriving(early, spans):
            c_proj(q, 1).wait_recv()


def per_device(samples, values, diag_entries, block_mask):
    height, order = values.shape
    count = samples.shape[0]
    groups = lax.axis_size("col")
    lines = lax.axis_size("row") // 4
    per_group = order // height
    block = groups * order // block_mask.shape[0]
    diag = diag_entries[None, :]
    anywhere = pl.BlockSpec(memory_space=pl.ANY)
    in_smem = pl.BlockSpec(memory_space=pltpu.SMEM)
    in_vmem = pl.BlockSpec(memory_space=VM)
    deep = min(64, count // 2)
    spans = count // deep
    early = spans // 2
    parts = max(1, min(PARTS, height // 128))
    chunks = spans * per_group * parts
    piece = deep // 8
    kinds = 16
    tile = min(2 * block, height)
    early_size = early * deep
    late_size = count - early_size
    flows = lambda *lead: VM((*lead, chunks, piece, height // parts), jnp.float32)
    dma = pltpu.SemaphoreType.DMA
    left, held = pl.pallas_call(
        functools.partial(reduce_kernel, lines, groups, per_group, early),
        out_shape=(
            VM((2 * count, height), jnp.float32),
            VM((height + count, order), jnp.float32),
        ),
        in_specs=[anywhere, anywhere, in_vmem, in_smem],
        out_specs=(in_vmem, in_vmem),
        scratch_shapes=[
            VM((chunks, deep // 2, height // parts), jnp.float32),
            flows(),
            flows(),
            flows(),
            flows(2),
            flows(2),
            flows(),
            dma((kinds,)),
            dma((chunks,)),
            dma((kinds, chunks)),
            VM((2 * count, height), jnp.bfloat16),
            VM((2, height, height), jnp.bfloat16),
            dma((per_group,)),
            dma((groups, spans)),
            dma((2, spans)),
            dma((groups, spans * parts)),
            dma((spans * parts,)),
            VM((height, 6 * early_size), jnp.bfloat16),
            VM((6 * early_size, tile), jnp.bfloat16),
            VM((2, early_size, tile), jnp.float32),
            dma((2,)),
        ],
        compiler_params=pltpu.CompilerParams(
            collective_id=1, has_side_effects=True, vmem_limit_bytes=REDUCE_LIMIT
        ),
    )(samples, values, diag, block_mask)

    left, held = (pltpu.with_memory_space_constraint(x, VM) for x in (left, held))
    return pl.pallas_call(
        functools.partial(update_kernel, early_size, per_group),
        out_shape=jax.ShapeDtypeStruct((height, order), jnp.float32),
        in_specs=[in_vmem, in_vmem, anywhere, in_vmem],
        out_specs=anywhere,
        scratch_shapes=[
            VM((height, 6 * late_size), jnp.bfloat16),
            VM((6 * late_size, tile), jnp.bfloat16),
            VM((2, late_size, tile), jnp.float32),
            VM((2, height, tile), jnp.float32),
            dma((2,)),
            dma((2,)),
        ],
        compiler_params=pltpu.CompilerParams(vmem_limit_bytes=UPDATE_LIMIT),
    )(left, held, samples, diag)


def solution(mesh):
    in_specs = (P(None, "col"), P("row", "col"), P("row"), P())
    out_specs = P("row", "col")
    return jax.shard_map(
        per_device, mesh=mesh, in_specs=in_specs, out_specs=out_specs, check_vma=False
    )
```

```python
import functools

import jax
import jax.numpy as jnp
from jax import lax
from jax.experimental import pallas as pl
from jax.experimental.pallas import tpu as pltpu
from jax.sharding import PartitionSpec as P

step_size = 8.0
penalty = 0.05
MESH = pl.DeviceIdType.MESH
VM = pltpu.VMEM
REDUCE_LIMIT = 21 * 1024 * 1024
UPDATE_LIMIT = 14 * 1024 * 1024
SLACK = 2
NEAR = 1


def split(x):
    high = x.astype(jnp.bfloat16)
    low = (x - high.astype(jnp.float32)).astype(jnp.bfloat16)
    return high, low


def dot(a, b):
    return jnp.dot(a, b, preferred_element_type=jnp.float32)


def on_diagonal(row_at, col_at, shape):
    rows = lax.broadcasted_iota(jnp.int32, shape, 0) + row_at
    cols = lax.broadcasted_iota(jnp.int32, shape, 1) + col_at
    return rows == cols


def masked(mask_ref, values, row_at, col_at, block):
    pieces = [
        values[:, at : at + block] * mask_ref[row_at // block, (col_at + at) // block].astype(jnp.float32)
        for at in range(0, values.shape[1], block)
    ]
    return jnp.concatenate(pieces, axis=1)


def crosses(row_at, col_at, shape):
    return jnp.logical_and(row_at < col_at + shape[1], col_at < row_at + shape[0])


def fill_lefts(lefts, left_ref, parts):
    count = left_ref.shape[0] // 2
    rows = jnp.concatenate([left_ref[first : first + size, :] for first, size in parts], axis=0)
    high, low = split(rows.T * (0.5 * step_size / count))
    lefts[:, :count] = high
    lefts[:, count : 2 * count] = low
    lefts[:, 2 * count :] = high


def fill_rights(rights, at, value):
    both = rights.shape[0] // 3
    high, low = split(value)
    rights[at : at + value.shape[0], :] = high
    rights[both + at : both + at + value.shape[0], :] = high
    rights[2 * both + at : 2 * both + at + value.shape[0], :] = low


def cross_of(lefts, rights, rows):
    return dot(lefts[rows, :], rights[...])


def update_kernel(
    per_group, deep, left_ref, held_ref, samples_ref, diag_ref, out_ref,
    lefts, rights, sample_tiles, out_tiles, sample_sem, out_sem,
):
    height, tile = out_tiles.shape[1:]
    count = left_ref.shape[0] // 2
    columns = held_ref.shape[1]
    width = columns // per_group
    steps = columns // tile
    most = count - deep
    row_at = lax.axis_index("row") * height
    col_base = lax.axis_index("col") * per_group * width
    block = height
    limit = step_size * penalty

    def columns_at(u):
        return pl.ds(pl.multiple_of(u * tile, tile), tile)

    def load(u):
        source = samples_ref.at[pl.ds(deep, most), columns_at(u)]
        return pltpu.make_async_copy(source, sample_tiles.at[u % 2], sample_sem.at[u % 2])

    def store(u):
        return pltpu.make_async_copy(out_tiles.at[u % 2], out_ref.at[:, columns_at(u)], out_sem.at[u % 2])

    load(0).start()
    load(1).start()
    fill_lefts(lefts, left_ref, [(most, deep), (count + deep, most)])

    @pl.loop(0, steps)
    def _(u):
        slot = u % 2
        load(u).wait()
        fill_rights(rights, 0, held_ref[height + most : height + count, columns_at(u)])
        fill_rights(rights, deep, sample_tiles[slot])
        pl.when(u + 2 < steps)(lambda: load(u + 2).start())
        pl.when(u >= 2)(lambda: store(u - 2).wait())
        col_at = col_base + u * tile

        def update(hit):
            for begin in range(0, height, block):
                rows = pl.ds(begin, block)
                stepped = held_ref[rows, columns_at(u)] - cross_of(lefts, rights, rows)
                new = stepped - jnp.clip(stepped, -limit, limit)
                if hit:
                    diag = diag_ref[:, pl.ds(pl.multiple_of(col_at - row_at, tile), tile)]
                    new = jnp.where(on_diagonal(row_at + begin, col_at, new.shape), stepped + step_size / diag, new)
                out_tiles[slot, rows, :] = new

        hit = crosses(row_at, col_at, (height, tile))
        pl.when(hit)(lambda: update(True))
        pl.when(jnp.logical_not(hit))(lambda: update(False))
        store(u).start()

    for u in range(max(0, steps - 2), steps):
        store(u).wait()


def reduce_kernel(
    lines, groups, per_group, samples_ref, values_ref, diag_ref, mask_ref, left_ref, held, *scratch
):
    core_in, y_in, a_in, a_mid, b_low, b_high, rung = scratch[:7]
    send, core_send, recv, lefts, rights, held_sem, fetch_send, fetch_sem, proj_send, proj_sem = scratch[7:17]
    early_lefts, early_rights, sample_tiles, sample_sem = scratch[17:]
    row, col = lax.axis_index("row"), lax.axis_index("col")
    core, side, line = row % 2, row // 2 % 2, row // 4
    last, middle = lines - 1, lines // 2
    core_mate = row + 1 - 2 * core
    y_mate = row + 2 - 4 * side
    up, down = row + 4, row - 4
    lower = line < middle
    inner = jnp.where(lower, up, down)
    outer = jnp.where(lower, down, up)
    depth = jnp.where(lower, line, last - line)
    is_mid = depth == middle - 1
    height, columns = values_ref.shape
    width = columns // per_group
    chunks, half, _ = core_in.shape
    deep, piece = 2 * half, half // 4
    spans = chunks // per_group
    inside = spans - 2
    samples = deep * spans
    block = groups * columns // mask_ref.shape[0]
    has_up, has_down = line < last, line > 0
    owner = row // per_group
    mine_at = row % per_group

    barrier = pltpu.get_barrier_semaphore()

    def greet(target):
        pl.semaphore_signal(barrier, inc=1, device_id=target, device_id_type=MESH)

    def load(i):
        cols = pl.ds(pl.multiple_of(i * width, width), width)
        return pltpu.make_async_copy(values_ref.at[:, cols], held.at[pl.ds(0, height), cols], held_sem.at[i])

    for i in range(2):
        load(i).start()
    greet((core_mate, col))
    greet((y_mate, col))
    pl.when(has_up)(lambda: greet((up, col)))
    pl.when(has_down)(lambda: greet((down, col)))
    for shift in range(1, groups):
        greet((row, lax.rem(col + shift, groups)))
    ends = jnp.where(has_up, 1, 0) + jnp.where(has_down, 1, 0)
    pl.semaphore_wait(barrier, 2 + groups - 1 + ends)

    def rows_at(at, size):
        return pl.ds(pl.multiple_of(at, piece), size)

    def copy(kind, q, source, target, device, landing=None):
        return pltpu.make_async_remote_copy(
            src_ref=source,
            dst_ref=target,
            send_sem=send.at[kind] if kind else core_send.at[q],
            recv_sem=recv.at[kind if landing is None else landing, q],
            device_id=(device, col),
            device_id_type=MESH,
        )

    def span_and_slice(q):
        k = jnp.maximum(q - per_group, 0)
        ending = q - per_group * (1 + inside)
        opens, ends = q < per_group, ending >= 0
        span = jnp.where(opens, 0, jnp.where(ends, spans - 1, 1 + k % inside))
        at = jnp.where(opens, q, jnp.where(ends, ending, k // inside))
        return span, at

    def place(q, at, size):
        span, slice_of = span_and_slice(q)
        return rows_at(height + span * deep + at, size), pl.ds(pl.multiple_of(slice_of * width, width), width)

    def spread(kind, q, at, size, device, landing=None):
        rows = held.at[place(q, at, size)]
        return copy(kind, q, rows, rows, device, landing)

    own_half = core * half
    b_own = [flow * piece for flow in range(2)]
    roots = [middle - 1, middle]
    a_own = 2 * piece + side * piece
    a_other = 2 * piece + (1 - side) * piece

    def c_core(q):
        return copy(0, q, held.at[place(q, (1 - core) * half, half)], core_in.at[q], core_mate)

    def c_y(q):
        return copy(1, q, core_in.at[q, rows_at(a_other, piece), :], y_in.at[q], y_mate)

    def c_a_in(q):
        return copy(2, q, y_in.at[q], a_in.at[q], inner)

    def c_a_mid(q):
        return copy(3, q, y_in.at[q], a_mid.at[q], inner)

    def c_a_out(q):
        return spread(4, q, own_half + a_own, piece, outer)

    def c_y_back(q):
        return spread(5, q, own_half + a_own, piece, y_mate)

    def y_back_arrival(q):
        return spread(5, q, own_half + a_other, piece, y_mate)

    def c_b_up(q, flow):
        return copy(6 + flow, q, core_in.at[q, rows_at(b_own[flow], piece), :], b_low.at[flow, q], up)

    def c_b_down(q, flow):
        return copy(8 + flow, q, core_in.at[q, rows_at(b_own[flow], piece), :], b_high.at[flow, q], down)

    def c_rung(q, flow):
        return copy(10, q, core_in.at[q, rows_at(b_own[flow], piece), :], rung.at[q], y_mate)

    def c_b_out(q, flow, upward):
        return spread(11 + 2 * flow + upward, q, own_half + b_own[flow], piece, up if upward else down, 11 + flow)

    def c_core_back(q):
        return spread(15, q, own_half, half, core_mate)

    def core_arrival(q):
        return spread(15, q, half - own_half, half, core_mate)

    def at_stage(t, offset, condition, action):
        q = t - offset
        live = jnp.logical_and(q >= 0, q < chunks)
        if condition is not None:
            live = jnp.logical_and(live, condition)
        pl.when(live)(lambda: action(jnp.clip(q, 0, chunks - 1)))

    def b_rows(flow):
        return pl.ds(b_own[flow], piece)

    def a_forward(q):
        pl.when(is_mid)(lambda: c_a_mid(q).start())
        pl.when(jnp.logical_not(is_mid))(lambda: c_a_in(q).start())

    def begin(q):
        c_core(q).wait()
        core_in[q] = core_in[q] + held[place(q, own_half, half)]
        c_y(q).start()
        for flow in range(2):
            if roots[flow] > 0:
                pl.when(line == 0)(lambda flow=flow: c_b_up(q, flow).start())
            if roots[flow] < last:
                pl.when(line == last)(lambda flow=flow: c_b_down(q, flow).start())

    def after_y(q):
        c_y(q).wait_recv()
        y_in[q] = y_in[q] + core_in[q, rows_at(a_own, piece), :]
        pl.when(depth == 0)(lambda: a_forward(q))

    def a_reduce(q):
        c_a_in(q).wait_recv()
        y_in[q] = y_in[q] + a_in[q]
        a_forward(q)

    def a_total(q):
        c_a_mid(q).wait_recv()
        held[place(q, own_half + a_own, piece)] = y_in[q] + a_mid[q]
        pl.when(depth > 0)(lambda: c_a_out(q).start())
        c_y_back(q).start()

    def a_back(q):
        c_a_out(q).wait_recv()
        pl.when(depth > 0)(lambda: c_a_out(q).start())
        c_y_back(q).start()

    def b_pass_up(q, flow):
        c_b_up(q, flow).wait_recv()
        core_in[q, b_rows(flow), :] = core_in[q, b_rows(flow), :] + b_low[flow, q]
        c_b_up(q, flow).start()

    def b_pass_down(q, flow):
        c_b_down(q, flow).wait_recv()
        core_in[q, b_rows(flow), :] = core_in[q, b_rows(flow), :] + b_high[flow, q]
        c_b_down(q, flow).start()

    def b_root(q, flow):
        if roots[flow] > 0:
            c_b_up(q, flow).wait_recv()
            core_in[q, b_rows(flow), :] = core_in[q, b_rows(flow), :] + b_low[flow, q]
        if roots[flow] < last:
            c_b_down(q, flow).wait_recv()
            core_in[q, b_rows(flow), :] = core_in[q, b_rows(flow), :] + b_high[flow, q]
        c_rung(q, flow).start()

    def b_total(q, flow):
        c_rung(q, flow).wait_recv()
        held[place(q, own_half + b_own[flow], piece)] = core_in[q, b_rows(flow), :] + rung[q]
        if roots[flow] > 0:
            c_b_out(q, flow, 0).start()
        if roots[flow] < last:
            c_b_out(q, flow, 1).start()

    def b_back(q, flow):
        c_b_out(q, flow, 0).wait_recv()
        pl.when(jnp.logical_and(line < roots[flow], has_down))(lambda: c_b_out(q, flow, 0).start())
        pl.when(jnp.logical_and(line > roots[flow], has_up))(lambda: c_b_out(q, flow, 1).start())

    def gather(q):
        y_back_arrival(q).wait_recv()
        c_core_back(q).start()

    def proj_rows(span):
        return pl.ds(pl.multiple_of(samples + span * deep, deep), deep)

    def c_proj(span, shift):
        cols = pl.ds(pl.multiple_of(mine_at * width, width), width)
        return pltpu.make_async_remote_copy(
            src_ref=held.at[pl.ds(pl.multiple_of(height + span * deep, deep), deep), cols],
            dst_ref=left_ref.at[proj_rows(span), :],
            send_sem=proj_send.at[shift, span],
            recv_sem=proj_sem.at[span],
            device_id=(row, lax.rem(col + shift, groups)),
            device_id_type=MESH,
        )

    is_owner = col == owner

    def finish(q):
        core_arrival(q).wait_recv()
        span, slice_of = span_and_slice(q)

        @pl.when(jnp.logical_and(is_owner, slice_of == mine_at))
        def _():
            for shift in range(1, groups):
                c_proj(span, shift).start()
            left_ref[proj_rows(span), :] = held[place(q, 0, deep)]

    slice_at = pl.multiple_of(mine_at * width, width)

    def fetched(span):
        rows = pl.ds(span * deep, deep)
        return samples_ref.at[rows, pl.ds(slice_at, width)], left_ref.at[rows, :]

    def fetch(shift, span):
        source, target = fetched(span)
        return pltpu.make_async_remote_copy(
            src_ref=source,
            dst_ref=target,
            send_sem=fetch_send.at[shift, span],
            recv_sem=fetch_sem.at[0, span],
            device_id=(row, lax.rem(col + shift, groups)),
            device_id_type=MESH,
        )

    def own(span):
        return pltpu.make_async_copy(*fetched(span), fetch_sem.at[1, span])

    @pl.when(is_owner)
    def _():
        for span in range(spans):
            for shift in range(1, groups):
                fetch(shift, span).start()
            own(span).start()

    def take(first, count):
        @pl.when(is_owner)
        def _():
            for span in range(first, first + count):
                own(span).wait()

        @pl.when(jnp.logical_not(is_owner))
        def _():
            for span in range(first, first + count):
                fetch(1, span).wait_recv()

        size = count * deep
        high, low = split(left_ref[pl.ds(first * deep, size), :])
        lefts[2 * first * deep : 2 * first * deep + size, :] = high
        lefts[2 * first * deep + size : 2 * (first * deep + size), :] = low

    def prepare_slice(span_at, fresh):
        if fresh:
            load(span_at).wait()
            pl.when(span_at + 2 < per_group)(lambda: load(span_at + 2).start())
        hit = jnp.logical_and(is_owner, span_at == mine_at)

        def put(k, b, omega):
            high, low = split(omega)
            rows, cols = pl.ds(k * block, block), pl.ds(b * block, block)
            rights[0, rows, cols] = high
            rights[1, rows, cols] = low

        def omega_at(k, b):
            cols = pl.ds(pl.multiple_of(span_at * width + b * block, block), block)
            mask_col = (col * columns + span_at * width) // block + b
            keep = mask_ref[row * height // block + k, mask_col].astype(jnp.float32)
            return held[k * block : (k + 1) * block, cols] * keep

        for b in range(width // block):
            for k in range(height // block):
                put(k, b, omega_at(k, b))

        @pl.when(hit)
        def _():
            for b in range(width // block):
                omega = omega_at(b, b)
                diag = diag_ref[:, b * block : (b + 1) * block]
                put(b, b, jnp.where(on_diagonal(0, 0, omega.shape), diag, omega))

    def project(span_at, first, count):
        size = count * deep
        base = 2 * first * deep
        both = dot(lefts[base : base + 2 * size, :], rights[0])
        total = both[:size, :] + both[size:, :] + dot(lefts[base : base + size, :], rights[1])
        cols = pl.ds(pl.multiple_of(span_at * width, width), width)
        held[height + first * deep : height + first * deep + size, cols] = total

    tile = sample_tiles.shape[2]
    steps = columns // tile
    most = samples - deep
    row_at = row * height

    def load_samples(u):
        cols = pl.ds(pl.multiple_of(u * tile, tile), tile)
        return pltpu.make_async_copy(
            samples_ref.at[pl.ds(0, deep), cols], sample_tiles.at[u % 2], sample_sem.at[u % 2]
        )

    def prepare():
        pl.when(jnp.logical_not(is_owner))(lambda: c_proj(0, 1).wait_recv())
        fill_lefts(early_lefts, left_ref, [(0, most), (samples, deep)])

    def step_early(u):
        cols = pl.ds(pl.multiple_of(u * tile, tile), tile)
        load_samples(u).wait()
        fill_rights(early_rights, 0, held[height : height + most, cols])
        fill_rights(early_rights, most, sample_tiles[u % 2])
        pl.when(u + 2 < steps)(lambda: load_samples(u + 2).start())
        col_at = col * columns + u * tile

        def update(hit):
            for begin_at in range(0, height, block):
                rows = pl.ds(begin_at, block)
                omega = masked(mask_ref, held[rows, cols], row_at + begin_at, col_at, block)
                if hit:
                    diag = diag_ref[:, pl.ds(pl.multiple_of(col_at - row_at, tile), tile)]
                    omega = jnp.where(on_diagonal(row_at + begin_at, col_at, omega.shape), diag, omega)
                held[rows, cols] = omega - cross_of(early_lefts, early_rights, rows)

        hit = crosses(row_at, col_at, (height, tile))
        pl.when(hit)(lambda: update(True))
        pl.when(jnp.logical_not(hit))(lambda: update(False))

    load_samples(0).start()
    load_samples(1).start()
    prepare_slice(0, True)
    take(0, 1)
    slack = SLACK
    near = NEAR

    depth_of_pipe = 2 * near + slack * (lines + 1)
    per_slice = width // tile
    early_at = per_group + max(inside, slack + 1) - 1 + depth_of_pipe

    @pl.loop(0, chunks + depth_of_pipe)
    def _(t):
        begin_t = t
        pl.when(t < per_group)(lambda: project(t, 0, 1))
        pl.when(t == per_group)(lambda: take(1, spans - 1))
        again = t - per_group

        @pl.when(jnp.logical_and(jnp.logical_and(again >= 0, again < inside * per_group), again % inside == 0))
        def _():
            project(again // inside, 1, spans - 1)

        at_stage(t, 0, None, lambda q: c_core(q).start())
        at_stage(t, near, None, begin)
        t = t - near
        at_stage(t, slack, None, after_y)
        for flow in range(2):
            root = roots[flow]
            if root > 1:
                at_stage(t, slack * line, jnp.logical_and(line > 0, line < root), lambda q, flow=flow: b_pass_up(q, flow))
            if root < last - 1:
                at_stage(t, slack * (last - line), jnp.logical_and(line > root, line < last), lambda q, flow=flow: b_pass_down(q, flow))
        if middle > 1:
            at_stage(t, slack * (1 + depth), depth > 0, a_reduce)
        for flow in range(2):
            at_stage(t, slack * middle, line == roots[flow], lambda q, flow=flow: b_root(q, flow))
        at_stage(t, slack * (1 + middle), is_mid, a_total)
        for flow in range(2):
            at_stage(t, slack * (1 + middle), line == roots[flow], lambda q, flow=flow: b_total(q, flow))
        if middle > 1:
            at_stage(t, slack * (lines - depth), jnp.logical_not(is_mid), a_back)
        for flow in range(2):
            away = jnp.abs(line - roots[flow])
            at_stage(t, slack * (1 + middle + away), away > 0, lambda q, flow=flow: b_back(q, flow))
        at_stage(t, slack * (lines + 1 - depth), None, gather)
        at_stage(t, near + slack * (lines + 1 - depth), None, finish)
        pl.when(begin_t == early_at)(prepare)
        pl.when(begin_t + 1 < per_group)(lambda: prepare_slice(begin_t + 1, True))
        following = begin_t + 1 - per_group

        @pl.when(
            jnp.logical_and(
                jnp.logical_and(following >= 0, following < inside * per_group), following % inside == 0
            )
        )
        def _():
            prepare_slice(following // inside, False)

        now = begin_t - early_at
        at_slice, turn = now // inside, now % inside
        live = jnp.logical_and(jnp.logical_and(now >= 0, at_slice < per_group), turn < per_slice)
        pl.when(live)(lambda: step_early(at_slice * per_slice + turn))

    def all_sent(kind, ref):
        copy(kind, 0, ref, ref, core_mate).wait_send()

    all_sent(1, y_in)
    pl.when(is_mid)(lambda: all_sent(3, y_in))
    pl.when(jnp.logical_not(is_mid))(lambda: all_sent(2, y_in))
    pl.when(depth > 0)(lambda: all_sent(4, y_in))
    all_sent(5, y_in)
    for flow in range(2):
        root = roots[flow]
        pl.when(line < root)(lambda flow=flow: all_sent(6 + flow, y_in))
        pl.when(line > root)(lambda flow=flow: all_sent(8 + flow, y_in))
        pl.when(line == root)(lambda: all_sent(10, y_in))
        pl.when(jnp.logical_and(line <= root, has_down))(lambda flow=flow: all_sent(11 + 2 * flow, y_in))
        pl.when(jnp.logical_and(line >= root, has_up))(lambda flow=flow: all_sent(12 + 2 * flow, y_in))
    all_sent(15, core_in)

    @pl.when(is_owner)
    def _():
        for span in range(spans):
            for shift in range(1, groups):
                fetch(shift, span).wait_send()
        for span in range(spans):
            for shift in range(1, groups):
                c_proj(span, shift).wait_send()

    @pl.when(jnp.logical_not(is_owner))
    def _():
        for span in range(1, spans):
            c_proj(span, 1).wait_recv()


def per_device(samples, values, diag_entries, block_mask):
    height, order = values.shape
    count = samples.shape[0]
    groups = lax.axis_size("col")
    lines = lax.axis_size("row") // 4
    per_group = order // height
    block = groups * order // block_mask.shape[0]
    diag = diag_entries[None, :]
    anywhere = pl.BlockSpec(memory_space=pl.ANY)
    in_smem = pl.BlockSpec(memory_space=pltpu.SMEM)
    in_vmem = pl.BlockSpec(memory_space=VM)
    deep = min(64, count // 2)
    spans = count // deep
    chunks = spans * per_group
    piece = deep // 8
    kinds = 16
    tile = min(2 * block, height)
    flows = lambda *lead: VM((*lead, chunks, piece, height), jnp.float32)
    dma = pltpu.SemaphoreType.DMA
    left, held = pl.pallas_call(
        functools.partial(reduce_kernel, lines, groups, per_group),
        out_shape=(
            VM((2 * count, height), jnp.float32),
            VM((height + count, order), jnp.float32),
        ),
        in_specs=[anywhere, anywhere, in_vmem, in_smem],
        out_specs=(in_vmem, in_vmem),
        scratch_shapes=[
            VM((chunks, deep // 2, height), jnp.float32),
            flows(),
            flows(),
            flows(),
            flows(2),
            flows(2),
            flows(),
            dma((kinds,)),
            dma((chunks,)),
            dma((kinds, chunks)),
            VM((2 * count, height), jnp.bfloat16),
            VM((2, height, height), jnp.bfloat16),
            dma((per_group,)),
            dma((groups, spans)),
            dma((2, spans)),
            dma((groups, spans)),
            dma((spans,)),
            VM((height, 3 * count), jnp.bfloat16),
            VM((3 * count, tile), jnp.bfloat16),
            VM((2, deep, tile), jnp.float32),
            dma((2,)),
        ],
        compiler_params=pltpu.CompilerParams(
            collective_id=1, has_side_effects=True, vmem_limit_bytes=REDUCE_LIMIT
        ),
    )(samples, values, diag, block_mask)

    left, held = (pltpu.with_memory_space_constraint(x, VM) for x in (left, held))
    return pl.pallas_call(
        functools.partial(update_kernel, per_group, deep),
        out_shape=jax.ShapeDtypeStruct((height, order), jnp.float32),
        in_specs=[in_vmem, in_vmem, anywhere, in_vmem],
        out_specs=anywhere,
        scratch_shapes=[
            VM((height, 3 * count), jnp.bfloat16),
            VM((3 * count, tile), jnp.bfloat16),
            VM((2, count - deep, tile), jnp.float32),
            VM((2, height, tile), jnp.float32),
            dma((2,)),
            dma((2,)),
        ],
        compiler_params=pltpu.CompilerParams(vmem_limit_bytes=UPDATE_LIMIT),
    )(left, held, samples, diag)


def solution(mesh):
    in_specs = (P(None, "col"), P("row", "col"), P("row"), P())
    out_specs = P("row", "col")
    return jax.shard_map(
        per_device, mesh=mesh, in_specs=in_specs, out_specs=out_specs, check_vma=False
    )
```

```python
import functools

import jax
import jax.numpy as jnp
from jax import lax
from jax.experimental import pallas as pl
from jax.experimental.pallas import tpu as pltpu
from jax.sharding import PartitionSpec as P

step_size = 8.0
penalty = 0.05
MESH = pl.DeviceIdType.MESH
VM = pltpu.VMEM
REDUCE_LIMIT = 21 * 1024 * 1024
UPDATE_LIMIT = 18 * 1024 * 1024
SLACK = 2
NEAR = 1
BLOCKS_DOWN = 4


def split(x):
    high = x.astype(jnp.bfloat16)
    low = (x - high.astype(jnp.float32)).astype(jnp.bfloat16)
    return high, low


def dot(a, b):
    return jnp.dot(a, b, preferred_element_type=jnp.float32)


def on_diagonal(row_at, col_at, shape):
    rows = lax.broadcasted_iota(jnp.int32, shape, 0) + row_at
    cols = lax.broadcasted_iota(jnp.int32, shape, 1) + col_at
    return rows == cols


def masked(mask_ref, values, row_at, col_at, block):
    pieces = [
        values[:, at : at + block] * mask_ref[row_at // block, (col_at + at) // block].astype(jnp.float32)
        for at in range(0, values.shape[1], block)
    ]
    return jnp.concatenate(pieces, axis=1)


def crosses(row_at, col_at, shape):
    return jnp.logical_and(row_at < col_at + shape[1], col_at < row_at + shape[0])


def fill_lefts(lefts, left_ref, parts):
    count = left_ref.shape[0] // 2
    rows = jnp.concatenate([left_ref[first : first + size, :] for first, size in parts], axis=0)
    high, low = split(rows.T * (0.5 * step_size / count))
    lefts[:, :count] = high
    lefts[:, count : 2 * count] = low
    lefts[:, 2 * count :] = high


def fill_rights(rights, at, value):
    both = rights.shape[0] // 3
    high, low = split(value)
    rights[at : at + value.shape[0], :] = high
    rights[both + at : both + at + value.shape[0], :] = high
    rights[2 * both + at : 2 * both + at + value.shape[0], :] = low


def cross_of(lefts, rights, rows):
    return dot(lefts[rows, :], rights[...])


def update_kernel(
    per_group, deep, left_ref, held_ref, samples_ref, diag_ref, out_ref,
    lefts, rights, sample_tiles, out_tiles, sample_sem, out_sem,
):
    height, tile = out_tiles.shape[1:]
    count = left_ref.shape[0] // 2
    columns = held_ref.shape[1]
    width = columns // per_group
    steps = columns // tile
    most = count - deep
    row_at = lax.axis_index("row") * height
    col_base = lax.axis_index("col") * per_group * width
    block = height // BLOCKS_DOWN
    limit = step_size * penalty

    def columns_at(u):
        return pl.ds(pl.multiple_of(u * tile, tile), tile)

    def load(u):
        source = samples_ref.at[pl.ds(deep, most), columns_at(u)]
        return pltpu.make_async_copy(source, sample_tiles.at[u % 2], sample_sem.at[u % 2])

    def store(u, at=0, size=height):
        rows = pl.ds(at, size)
        return pltpu.make_async_copy(
            out_tiles.at[u % 2, rows, :], out_ref.at[rows, columns_at(u)], out_sem.at[u % 2]
        )

    load(0).start()
    load(1).start()
    fill_lefts(lefts, left_ref, [(most, deep), (count + deep, most)])

    @pl.loop(0, steps)
    def _(u):
        slot = u % 2
        load(u).wait()
        fill_rights(rights, 0, held_ref[height + most : height + count, columns_at(u)])
        fill_rights(rights, deep, sample_tiles[slot])
        pl.when(u + 2 < steps)(lambda: load(u + 2).start())
        pl.when(u >= 2)(lambda: store(u - 2).wait())
        col_at = col_base + u * tile

        def update(hit):
            for begin in range(0, height, block):
                rows = pl.ds(begin, block)
                stepped = held_ref[rows, columns_at(u)] - cross_of(lefts, rights, rows)
                new = stepped - jnp.clip(stepped, -limit, limit)
                if hit:
                    diag = diag_ref[:, pl.ds(pl.multiple_of(col_at - row_at, tile), tile)]
                    new = jnp.where(on_diagonal(row_at + begin, col_at, new.shape), stepped + step_size / diag, new)
                out_tiles[slot, rows, :] = new
                store(u, begin, block).start()

        hit = crosses(row_at, col_at, (height, tile))
        pl.when(hit)(lambda: update(True))
        pl.when(jnp.logical_not(hit))(lambda: update(False))

    for u in range(max(0, steps - 2), steps):
        store(u).wait()


def reduce_kernel(
    lines, groups, per_group, samples_ref, values_ref, diag_ref, mask_ref, left_ref, held, *scratch
):
    core_in, y_in, a_in, a_mid, b_low, b_high, rung = scratch[:7]
    send, core_send, recv, lefts, rights, held_sem, fetch_send, fetch_sem, proj_send, proj_sem = scratch[7:17]
    early_lefts, early_rights, sample_tiles, sample_sem = scratch[17:]
    row, col = lax.axis_index("row"), lax.axis_index("col")
    core, side, line = row % 2, row // 2 % 2, row // 4
    last, middle = lines - 1, lines // 2
    core_mate = row + 1 - 2 * core
    y_mate = row + 2 - 4 * side
    up, down = row + 4, row - 4
    lower = line < middle
    inner = jnp.where(lower, up, down)
    outer = jnp.where(lower, down, up)
    depth = jnp.where(lower, line, last - line)
    is_mid = depth == middle - 1
    height, columns = values_ref.shape
    width = columns // per_group
    chunks, half, _ = core_in.shape
    deep, piece = 2 * half, half // 4
    spans = chunks // per_group
    inside = spans - 2
    samples = deep * spans
    block = groups * columns // mask_ref.shape[0]
    has_up, has_down = line < last, line > 0
    owner = row // per_group
    mine_at = row % per_group

    barrier = pltpu.get_barrier_semaphore()

    def greet(target):
        pl.semaphore_signal(barrier, inc=1, device_id=target, device_id_type=MESH)

    def load(i):
        cols = pl.ds(pl.multiple_of(i * width, width), width)
        return pltpu.make_async_copy(values_ref.at[:, cols], held.at[pl.ds(0, height), cols], held_sem.at[i])

    for i in range(2):
        load(i).start()
    greet((core_mate, col))
    greet((y_mate, col))
    pl.when(has_up)(lambda: greet((up, col)))
    pl.when(has_down)(lambda: greet((down, col)))
    for shift in range(1, groups):
        greet((row, lax.rem(col + shift, groups)))
    ends = jnp.where(has_up, 1, 0) + jnp.where(has_down, 1, 0)
    pl.semaphore_wait(barrier, 2 + groups - 1 + ends)

    def rows_at(at, size):
        return pl.ds(pl.multiple_of(at, piece), size)

    def copy(kind, q, source, target, device, landing=None):
        return pltpu.make_async_remote_copy(
            src_ref=source,
            dst_ref=target,
            send_sem=send.at[kind] if kind else core_send.at[q],
            recv_sem=recv.at[kind if landing is None else landing, q],
            device_id=(device, col),
            device_id_type=MESH,
        )

    def span_and_slice(q):
        k = jnp.maximum(q - per_group, 0)
        ending = q - per_group * (1 + inside)
        opens, ends = q < per_group, ending >= 0
        span = jnp.where(opens, 0, jnp.where(ends, spans - 1, 1 + k % inside))
        at = jnp.where(opens, q, jnp.where(ends, ending, k // inside))
        return span, at

    def place(q, at, size):
        span, slice_of = span_and_slice(q)
        return rows_at(height + span * deep + at, size), pl.ds(pl.multiple_of(slice_of * width, width), width)

    def spread(kind, q, at, size, device, landing=None):
        rows = held.at[place(q, at, size)]
        return copy(kind, q, rows, rows, device, landing)

    own_half = core * half
    b_own = [flow * piece for flow in range(2)]
    roots = [middle - 1, middle]
    a_own = 2 * piece + side * piece
    a_other = 2 * piece + (1 - side) * piece

    def c_core(q):
        return copy(0, q, held.at[place(q, (1 - core) * half, half)], core_in.at[q], core_mate)

    def c_y(q):
        return copy(1, q, core_in.at[q, rows_at(a_other, piece), :], y_in.at[q], y_mate)

    def c_a_in(q):
        return copy(2, q, y_in.at[q], a_in.at[q], inner)

    def c_a_mid(q):
        return copy(3, q, y_in.at[q], a_mid.at[q], inner)

    def c_a_out(q):
        return spread(4, q, own_half + a_own, piece, outer)

    def c_y_back(q):
        return spread(5, q, own_half + a_own, piece, y_mate)

    def y_back_arrival(q):
        return spread(5, q, own_half + a_other, piece, y_mate)

    def c_b_up(q, flow):
        return copy(6 + flow, q, core_in.at[q, rows_at(b_own[flow], piece), :], b_low.at[flow, q], up)

    def c_b_down(q, flow):
        return copy(8 + flow, q, core_in.at[q, rows_at(b_own[flow], piece), :], b_high.at[flow, q], down)

    def c_rung(q, flow):
        return copy(10, q, core_in.at[q, rows_at(b_own[flow], piece), :], rung.at[q], y_mate)

    def c_b_out(q, flow, upward):
        return spread(11 + 2 * flow + upward, q, own_half + b_own[flow], piece, up if upward else down, 11 + flow)

    def c_core_back(q):
        return spread(15, q, own_half, half, core_mate)

    def core_arrival(q):
        return spread(15, q, half - own_half, half, core_mate)

    def at_stage(t, offset, condition, action):
        q = t - offset
        live = jnp.logical_and(q >= 0, q < chunks)
        if condition is not None:
            live = jnp.logical_and(live, condition)
        pl.when(live)(lambda: action(jnp.clip(q, 0, chunks - 1)))

    def b_rows(flow):
        return pl.ds(b_own[flow], piece)

    def a_forward(q):
        pl.when(is_mid)(lambda: c_a_mid(q).start())
        pl.when(jnp.logical_not(is_mid))(lambda: c_a_in(q).start())

    def begin(q):
        c_core(q).wait()
        core_in[q] = core_in[q] + held[place(q, own_half, half)]
        c_y(q).start()
        for flow in range(2):
            if roots[flow] > 0:
                pl.when(line == 0)(lambda flow=flow: c_b_up(q, flow).start())
            if roots[flow] < last:
                pl.when(line == last)(lambda flow=flow: c_b_down(q, flow).start())

    def after_y(q):
        c_y(q).wait_recv()
        y_in[q] = y_in[q] + core_in[q, rows_at(a_own, piece), :]
        pl.when(depth == 0)(lambda: a_forward(q))

    def a_reduce(q):
        c_a_in(q).wait_recv()
        y_in[q] = y_in[q] + a_in[q]
        a_forward(q)

    def a_total(q):
        c_a_mid(q).wait_recv()
        held[place(q, own_half + a_own, piece)] = y_in[q] + a_mid[q]
        pl.when(depth > 0)(lambda: c_a_out(q).start())
        c_y_back(q).start()

    def a_back(q):
        c_a_out(q).wait_recv()
        pl.when(depth > 0)(lambda: c_a_out(q).start())
        c_y_back(q).start()

    def b_pass_up(q, flow):
        c_b_up(q, flow).wait_recv()
        core_in[q, b_rows(flow), :] = core_in[q, b_rows(flow), :] + b_low[flow, q]
        c_b_up(q, flow).start()

    def b_pass_down(q, flow):
        c_b_down(q, flow).wait_recv()
        core_in[q, b_rows(flow), :] = core_in[q, b_rows(flow), :] + b_high[flow, q]
        c_b_down(q, flow).start()

    def b_root(q, flow):
        if roots[flow] > 0:
            c_b_up(q, flow).wait_recv()
            core_in[q, b_rows(flow), :] = core_in[q, b_rows(flow), :] + b_low[flow, q]
        if roots[flow] < last:
            c_b_down(q, flow).wait_recv()
            core_in[q, b_rows(flow), :] = core_in[q, b_rows(flow), :] + b_high[flow, q]
        c_rung(q, flow).start()

    def b_total(q, flow):
        c_rung(q, flow).wait_recv()
        held[place(q, own_half + b_own[flow], piece)] = core_in[q, b_rows(flow), :] + rung[q]
        if roots[flow] > 0:
            c_b_out(q, flow, 0).start()
        if roots[flow] < last:
            c_b_out(q, flow, 1).start()

    def b_back(q, flow):
        c_b_out(q, flow, 0).wait_recv()
        pl.when(jnp.logical_and(line < roots[flow], has_down))(lambda: c_b_out(q, flow, 0).start())
        pl.when(jnp.logical_and(line > roots[flow], has_up))(lambda: c_b_out(q, flow, 1).start())

    def gather(q):
        y_back_arrival(q).wait_recv()
        c_core_back(q).start()

    def proj_rows(span):
        return pl.ds(pl.multiple_of(samples + span * deep, deep), deep)

    def c_proj(span, shift):
        cols = pl.ds(pl.multiple_of(mine_at * width, width), width)
        return pltpu.make_async_remote_copy(
            src_ref=held.at[pl.ds(pl.multiple_of(height + span * deep, deep), deep), cols],
            dst_ref=left_ref.at[proj_rows(span), :],
            send_sem=proj_send.at[shift, span],
            recv_sem=proj_sem.at[span],
            device_id=(row, lax.rem(col + shift, groups)),
            device_id_type=MESH,
        )

    is_owner = col == owner

    def finish(q):
        core_arrival(q).wait_recv()
        span, slice_of = span_and_slice(q)

        @pl.when(jnp.logical_and(is_owner, slice_of == mine_at))
        def _():
            for shift in range(1, groups):
                c_proj(span, shift).start()
            left_ref[proj_rows(span), :] = held[place(q, 0, deep)]

    slice_at = pl.multiple_of(mine_at * width, width)

    def fetched(span):
        rows = pl.ds(span * deep, deep)
        return samples_ref.at[rows, pl.ds(slice_at, width)], left_ref.at[rows, :]

    def fetch(shift, span):
        source, target = fetched(span)
        return pltpu.make_async_remote_copy(
            src_ref=source,
            dst_ref=target,
            send_sem=fetch_send.at[shift, span],
            recv_sem=fetch_sem.at[0, span],
            device_id=(row, lax.rem(col + shift, groups)),
            device_id_type=MESH,
        )

    def own(span):
        return pltpu.make_async_copy(*fetched(span), fetch_sem.at[1, span])

    @pl.when(is_owner)
    def _():
        for span in range(spans):
            for shift in range(1, groups):
                fetch(shift, span).start()
            own(span).start()

    def take(first, count):
        @pl.when(is_owner)
        def _():
            for span in range(first, first + count):
                own(span).wait()

        @pl.when(jnp.logical_not(is_owner))
        def _():
            for span in range(first, first + count):
                fetch(1, span).wait_recv()

        size = count * deep
        high, low = split(left_ref[pl.ds(first * deep, size), :])
        lefts[2 * first * deep : 2 * first * deep + size, :] = high
        lefts[2 * first * deep + size : 2 * (first * deep + size), :] = low

    def prepare_slice(span_at, fresh):
        if fresh:
            load(span_at).wait()
            pl.when(span_at + 2 < per_group)(lambda: load(span_at + 2).start())
        hit = jnp.logical_and(is_owner, span_at == mine_at)

        def put(k, b, omega):
            high, low = split(omega)
            rows, cols = pl.ds(k * block, block), pl.ds(b * block, block)
            rights[0, rows, cols] = high
            rights[1, rows, cols] = low

        def omega_at(k, b):
            cols = pl.ds(pl.multiple_of(span_at * width + b * block, block), block)
            mask_col = (col * columns + span_at * width) // block + b
            keep = mask_ref[row * height // block + k, mask_col].astype(jnp.float32)
            return held[k * block : (k + 1) * block, cols] * keep

        for b in range(width // block):
            for k in range(height // block):
                put(k, b, omega_at(k, b))

        @pl.when(hit)
        def _():
            for b in range(width // block):
                omega = omega_at(b, b)
                diag = diag_ref[:, b * block : (b + 1) * block]
                put(b, b, jnp.where(on_diagonal(0, 0, omega.shape), diag, omega))

    def project(span_at, first, count):
        size = count * deep
        base = 2 * first * deep
        both = dot(lefts[base : base + 2 * size, :], rights[0])
        total = both[:size, :] + both[size:, :] + dot(lefts[base : base + size, :], rights[1])
        cols = pl.ds(pl.multiple_of(span_at * width, width), width)
        held[height + first * deep : height + first * deep + size, cols] = total

    tile = sample_tiles.shape[2]
    steps = columns // tile
    most = samples - deep
    row_at = row * height

    def load_samples(u):
        cols = pl.ds(pl.multiple_of(u * tile, tile), tile)
        return pltpu.make_async_copy(
            samples_ref.at[pl.ds(0, deep), cols], sample_tiles.at[u % 2], sample_sem.at[u % 2]
        )

    def prepare():
        pl.when(jnp.logical_not(is_owner))(lambda: c_proj(0, 1).wait_recv())
        fill_lefts(early_lefts, left_ref, [(0, most), (samples, deep)])

    def step_early(u):
        cols = pl.ds(pl.multiple_of(u * tile, tile), tile)
        load_samples(u).wait()
        fill_rights(early_rights, 0, held[height : height + most, cols])
        fill_rights(early_rights, most, sample_tiles[u % 2])
        pl.when(u + 2 < steps)(lambda: load_samples(u + 2).start())
        col_at = col * columns + u * tile

        def update(hit):
            for begin_at in range(0, height, block):
                rows = pl.ds(begin_at, block)
                omega = masked(mask_ref, held[rows, cols], row_at + begin_at, col_at, block)
                if hit:
                    diag = diag_ref[:, pl.ds(pl.multiple_of(col_at - row_at, tile), tile)]
                    omega = jnp.where(on_diagonal(row_at + begin_at, col_at, omega.shape), diag, omega)
                held[rows, cols] = omega - cross_of(early_lefts, early_rights, rows)

        hit = crosses(row_at, col_at, (height, tile))
        pl.when(hit)(lambda: update(True))
        pl.when(jnp.logical_not(hit))(lambda: update(False))

    load_samples(0).start()
    load_samples(1).start()
    prepare_slice(0, True)
    take(0, 1)
    slack = SLACK
    near = NEAR

    depth_of_pipe = 2 * near + slack * (lines + 1)
    per_slice = width // tile
    early_at = per_group + max(inside, slack + 1) - 1 + depth_of_pipe

    @pl.loop(0, chunks + depth_of_pipe)
    def _(t):
        begin_t = t
        t = begin_t - near
        at_stage(t, near + slack * (lines + 1 - depth), None, finish)
        for flow in range(2):
            away = jnp.abs(line - roots[flow])
            at_stage(t, slack * (1 + middle + away), away > 0, lambda q, flow=flow: b_back(q, flow))
        at_stage(t, slack * (lines + 1 - depth), None, gather)
        if middle > 1:
            at_stage(t, slack * (lines - depth), jnp.logical_not(is_mid), a_back)
        for flow in range(2):
            at_stage(t, slack * (1 + middle), line == roots[flow], lambda q, flow=flow: b_total(q, flow))
        at_stage(t, slack * (1 + middle), is_mid, a_total)
        for flow in range(2):
            at_stage(t, slack * middle, line == roots[flow], lambda q, flow=flow: b_root(q, flow))
        if middle > 1:
            at_stage(t, slack * (1 + depth), depth > 0, a_reduce)
        for flow in range(2):
            root = roots[flow]
            if root > 1:
                at_stage(t, slack * line, jnp.logical_and(line > 0, line < root), lambda q, flow=flow: b_pass_up(q, flow))
            if root < last - 1:
                at_stage(t, slack * (last - line), jnp.logical_and(line > root, line < last), lambda q, flow=flow: b_pass_down(q, flow))
        at_stage(t, slack, None, after_y)
        at_stage(t, 0, None, begin)
        t = begin_t
        pl.when(t < per_group)(lambda: project(t, 0, 1))
        pl.when(t == per_group)(lambda: take(1, spans - 1))
        again = t - per_group

        @pl.when(jnp.logical_and(jnp.logical_and(again >= 0, again < inside * per_group), again % inside == 0))
        def _():
            project(again // inside, 1, spans - 1)

        at_stage(t, 0, None, lambda q: c_core(q).start())
        pl.when(begin_t == early_at)(prepare)
        pl.when(begin_t + 1 < per_group)(lambda: prepare_slice(begin_t + 1, True))
        following = begin_t + 1 - per_group

        @pl.when(
            jnp.logical_and(
                jnp.logical_and(following >= 0, following < inside * per_group), following % inside == 0
            )
        )
        def _():
            prepare_slice(following // inside, False)

        now = begin_t - early_at
        at_slice, turn = now // inside, now % inside
        live = jnp.logical_and(jnp.logical_and(now >= 0, at_slice < per_group), turn < per_slice)
        pl.when(live)(lambda: step_early(at_slice * per_slice + turn))

    def all_sent(kind, ref):
        copy(kind, 0, ref, ref, core_mate).wait_send()

    all_sent(1, y_in)
    pl.when(is_mid)(lambda: all_sent(3, y_in))
    pl.when(jnp.logical_not(is_mid))(lambda: all_sent(2, y_in))
    pl.when(depth > 0)(lambda: all_sent(4, y_in))
    all_sent(5, y_in)
    for flow in range(2):
        root = roots[flow]
        pl.when(line < root)(lambda flow=flow: all_sent(6 + flow, y_in))
        pl.when(line > root)(lambda flow=flow: all_sent(8 + flow, y_in))
        pl.when(line == root)(lambda: all_sent(10, y_in))
        pl.when(jnp.logical_and(line <= root, has_down))(lambda flow=flow: all_sent(11 + 2 * flow, y_in))
        pl.when(jnp.logical_and(line >= root, has_up))(lambda flow=flow: all_sent(12 + 2 * flow, y_in))
    all_sent(15, core_in)

    @pl.when(is_owner)
    def _():
        for span in range(spans):
            for shift in range(1, groups):
                fetch(shift, span).wait_send()
        for span in range(spans):
            for shift in range(1, groups):
                c_proj(span, shift).wait_send()

    @pl.when(jnp.logical_not(is_owner))
    def _():
        for span in range(1, spans):
            c_proj(span, 1).wait_recv()


def per_device(samples, values, diag_entries, block_mask):
    height, order = values.shape
    count = samples.shape[0]
    groups = lax.axis_size("col")
    lines = lax.axis_size("row") // 4
    per_group = order // height
    block = groups * order // block_mask.shape[0]
    diag = diag_entries[None, :]
    anywhere = pl.BlockSpec(memory_space=pl.ANY)
    in_smem = pl.BlockSpec(memory_space=pltpu.SMEM)
    in_vmem = pl.BlockSpec(memory_space=VM)
    deep = min(64, count // 2)
    spans = count // deep
    chunks = spans * per_group
    piece = deep // 8
    kinds = 16
    tile = min(2 * block, height)
    flows = lambda *lead: VM((*lead, chunks, piece, height), jnp.float32)
    dma = pltpu.SemaphoreType.DMA
    left, held = pl.pallas_call(
        functools.partial(reduce_kernel, lines, groups, per_group),
        out_shape=(
            VM((2 * count, height), jnp.float32),
            VM((height + count, order), jnp.float32),
        ),
        in_specs=[anywhere, anywhere, in_vmem, in_smem],
        out_specs=(in_vmem, in_vmem),
        scratch_shapes=[
            VM((chunks, deep // 2, height), jnp.float32),
            flows(),
            flows(),
            flows(),
            flows(2),
            flows(2),
            flows(),
            dma((kinds,)),
            dma((chunks,)),
            dma((kinds, chunks)),
            VM((2 * count, height), jnp.bfloat16),
            VM((2, height, height), jnp.bfloat16),
            dma((per_group,)),
            dma((groups, spans)),
            dma((2, spans)),
            dma((groups, spans)),
            dma((spans,)),
            VM((height, 3 * count), jnp.bfloat16),
            VM((3 * count, tile), jnp.bfloat16),
            VM((2, deep, tile), jnp.float32),
            dma((2,)),
        ],
        compiler_params=pltpu.CompilerParams(
            collective_id=1, has_side_effects=True, vmem_limit_bytes=REDUCE_LIMIT
        ),
    )(samples, values, diag, block_mask)

    left, held = (pltpu.with_memory_space_constraint(x, VM) for x in (left, held))
    wide = min(4 * block, height)
    return pl.pallas_call(
        functools.partial(update_kernel, per_group, deep),
        out_shape=jax.ShapeDtypeStruct((height, order), jnp.float32),
        in_specs=[in_vmem, in_vmem, anywhere, in_vmem],
        out_specs=anywhere,
        scratch_shapes=[
            VM((height, 3 * count), jnp.bfloat16),
            VM((3 * count, wide), jnp.bfloat16),
            VM((2, count - deep, wide), jnp.float32),
            VM((2, height, wide), jnp.float32),
            dma((2,)),
            dma((2,)),
        ],
        compiler_params=pltpu.CompilerParams(vmem_limit_bytes=UPDATE_LIMIT),
    )(left, held, samples, diag)


def solution(mesh):
    in_specs = (P(None, "col"), P("row", "col"), P("row"), P())
    out_specs = P("row", "col")
    return jax.shard_map(
        per_device, mesh=mesh, in_specs=in_specs, out_specs=out_specs, check_vma=False
    )
```

```python
import functools

import jax
import jax.numpy as jnp
from jax import lax
from jax.experimental import pallas as pl
from jax.experimental.pallas import tpu as pltpu
from jax.sharding import PartitionSpec as P

step_size = 8.0
penalty = 0.05
MESH = pl.DeviceIdType.MESH
VM = pltpu.VMEM
REDUCE_LIMIT = 21 * 1024 * 1024
UPDATE_LIMIT = 18 * 1024 * 1024
SLACK = 2
NEAR = 1
BLOCKS_DOWN = 4


def split(x):
    high = x.astype(jnp.bfloat16)
    low = (x - high.astype(jnp.float32)).astype(jnp.bfloat16)
    return high, low


def dot(a, b):
    return jnp.dot(a, b, preferred_element_type=jnp.float32)


def on_diagonal(row_at, col_at, shape):
    rows = lax.broadcasted_iota(jnp.int32, shape, 0) + row_at
    cols = lax.broadcasted_iota(jnp.int32, shape, 1) + col_at
    return rows == cols


def masked(mask_ref, values, row_at, col_at, block):
    pieces = [
        values[:, at : at + block] * mask_ref[row_at // block, (col_at + at) // block].astype(jnp.float32)
        for at in range(0, values.shape[1], block)
    ]
    return jnp.concatenate(pieces, axis=1)


def crosses(row_at, col_at, shape):
    return jnp.logical_and(row_at < col_at + shape[1], col_at < row_at + shape[0])


def fill_lefts(lefts, left_ref, parts):
    count = left_ref.shape[0] // 2
    rows = jnp.concatenate([left_ref[first : first + size, :] for first, size in parts], axis=0)
    high, low = split(rows.T * (0.5 * step_size / count))
    lefts[:, :count] = high
    lefts[:, count : 2 * count] = low
    lefts[:, 2 * count :] = high


def fill_rights(rights, at, value):
    both = rights.shape[0] // 3
    high, low = split(value)
    rights[at : at + value.shape[0], :] = high
    rights[both + at : both + at + value.shape[0], :] = high
    rights[2 * both + at : 2 * both + at + value.shape[0], :] = low


def cross_of(lefts, rights, rows):
    return dot(lefts[rows, :], rights[...])


def update_kernel(
    per_group, deep, left_ref, held_ref, samples_ref, diag_ref, out_ref,
    lefts, rights, sample_tiles, out_tiles, sample_sem, out_sem,
):
    height, tile = out_tiles.shape[1:]
    count = left_ref.shape[0] // 2
    columns = held_ref.shape[1]
    width = columns // per_group
    steps = columns // tile
    most = count - deep
    row_at = lax.axis_index("row") * height
    col_base = lax.axis_index("col") * per_group * width
    block = height // BLOCKS_DOWN
    limit = step_size * penalty

    def columns_at(u):
        return pl.ds(pl.multiple_of(u * tile, tile), tile)

    def load(u):
        source = samples_ref.at[pl.ds(deep, most), columns_at(u)]
        return pltpu.make_async_copy(source, sample_tiles.at[u % 2], sample_sem.at[u % 2])

    def store(u, at=0, size=height):
        rows = pl.ds(at, size)
        return pltpu.make_async_copy(
            out_tiles.at[u % 2, rows, :], out_ref.at[rows, columns_at(u)], out_sem.at[u % 2]
        )

    load(0).start()
    load(1).start()
    fill_lefts(lefts, left_ref, [(most, deep), (count + deep, most)])

    @pl.loop(0, steps)
    def _(u):
        slot = u % 2
        load(u).wait()
        fill_rights(rights, 0, held_ref[height + most : height + count, columns_at(u)])
        fill_rights(rights, deep, sample_tiles[slot])
        pl.when(u + 2 < steps)(lambda: load(u + 2).start())
        pl.when(u >= 2)(lambda: store(u - 2).wait())
        col_at = col_base + u * tile

        def update(hit):
            for begin in range(0, height, block):
                rows = pl.ds(begin, block)
                stepped = held_ref[rows, columns_at(u)] - cross_of(lefts, rights, rows)
                new = stepped - jnp.clip(stepped, -limit, limit)
                if hit:
                    diag = diag_ref[:, pl.ds(pl.multiple_of(col_at - row_at, tile), tile)]
                    new = jnp.where(on_diagonal(row_at + begin, col_at, new.shape), stepped + step_size / diag, new)
                out_tiles[slot, rows, :] = new
                store(u, begin, block).start()

        hit = crosses(row_at, col_at, (height, tile))
        pl.when(hit)(lambda: update(True))
        pl.when(jnp.logical_not(hit))(lambda: update(False))

    for u in range(max(0, steps - 2), steps):
        store(u).wait()


def reduce_kernel(
    lines, groups, per_group, samples_ref, values_ref, diag_ref, mask_ref, left_ref, held, *scratch
):
    core_in, y_in, a_in, a_mid, b_low, b_high, rung = scratch[:7]
    send, core_send, recv, lefts, rights, held_sem, fetch_send, fetch_sem, proj_send, proj_sem = scratch[7:17]
    early_lefts, early_rights, sample_tiles, sample_sem = scratch[17:]
    row, col = lax.axis_index("row"), lax.axis_index("col")
    core, side, line = row % 2, row // 2 % 2, row // 4
    last, middle = lines - 1, lines // 2
    core_mate = row + 1 - 2 * core
    y_mate = row + 2 - 4 * side
    up, down = row + 4, row - 4
    lower = line < middle
    inner = jnp.where(lower, up, down)
    outer = jnp.where(lower, down, up)
    depth = jnp.where(lower, line, last - line)
    is_mid = depth == middle - 1
    height, columns = values_ref.shape
    width = columns // per_group
    chunks, half, _ = core_in.shape
    deep, piece = 2 * half, half // 4
    spans = chunks // per_group
    inside = spans - 2
    samples = deep * spans
    block = groups * columns // mask_ref.shape[0]
    has_up, has_down = line < last, line > 0
    owner = row // per_group
    mine_at = row % per_group

    barrier = pltpu.get_barrier_semaphore()

    def greet(target):
        pl.semaphore_signal(barrier, inc=1, device_id=target, device_id_type=MESH)

    def load(i):
        cols = pl.ds(pl.multiple_of(i * width, width), width)
        return pltpu.make_async_copy(values_ref.at[:, cols], held.at[pl.ds(0, height), cols], held_sem.at[i])

    for i in range(2):
        load(i).start()
    greet((core_mate, col))
    greet((y_mate, col))
    pl.when(has_up)(lambda: greet((up, col)))
    pl.when(has_down)(lambda: greet((down, col)))
    for shift in range(1, groups):
        greet((row, lax.rem(col + shift, groups)))
    ends = jnp.where(has_up, 1, 0) + jnp.where(has_down, 1, 0)
    pl.semaphore_wait(barrier, 2 + groups - 1 + ends)

    def rows_at(at, size):
        return pl.ds(pl.multiple_of(at, piece), size)

    def copy(kind, q, source, target, device, landing=None):
        return pltpu.make_async_remote_copy(
            src_ref=source,
            dst_ref=target,
            send_sem=send.at[kind] if kind else core_send.at[q],
            recv_sem=recv.at[kind if landing is None else landing, q],
            device_id=(device, col),
            device_id_type=MESH,
        )

    def span_and_slice(q):
        k = jnp.maximum(q - per_group, 0)
        ending = q - per_group * (1 + inside)
        opens, ends = q < per_group, ending >= 0
        span = jnp.where(opens, 0, jnp.where(ends, spans - 1, 1 + k % inside))
        at = jnp.where(opens, q, jnp.where(ends, ending, k // inside))
        return span, at

    def place(q, at, size):
        span, slice_of = span_and_slice(q)
        return rows_at(height + span * deep + at, size), pl.ds(pl.multiple_of(slice_of * width, width), width)

    def spread(kind, q, at, size, device, landing=None):
        rows = held.at[place(q, at, size)]
        return copy(kind, q, rows, rows, device, landing)

    own_half = core * half
    b_own = [flow * piece for flow in range(2)]
    roots = [middle - 1, middle]
    a_own = 2 * piece + side * piece
    a_other = 2 * piece + (1 - side) * piece

    def c_core(q):
        return copy(0, q, held.at[place(q, (1 - core) * half, half)], core_in.at[q], core_mate)

    def c_y(q):
        return copy(1, q, core_in.at[q, rows_at(a_other, piece), :], y_in.at[q], y_mate)

    def c_a_in(q):
        return copy(2, q, y_in.at[q], a_in.at[q], inner)

    def c_a_mid(q):
        return copy(3, q, y_in.at[q], a_mid.at[q], inner)

    def c_a_out(q):
        return spread(4, q, own_half + a_own, piece, outer)

    def c_y_back(q):
        return spread(5, q, own_half + a_own, piece, y_mate)

    def y_back_arrival(q):
        return spread(5, q, own_half + a_other, piece, y_mate)

    def c_b_up(q, flow):
        return copy(6 + flow, q, core_in.at[q, rows_at(b_own[flow], piece), :], b_low.at[flow, q], up)

    def c_b_down(q, flow):
        return copy(8 + flow, q, core_in.at[q, rows_at(b_own[flow], piece), :], b_high.at[flow, q], down)

    def c_rung(q, flow):
        return copy(10, q, core_in.at[q, rows_at(b_own[flow], piece), :], rung.at[q], y_mate)

    def c_b_out(q, flow, upward):
        return spread(11 + 2 * flow + upward, q, own_half + b_own[flow], piece, up if upward else down, 11 + flow)

    def c_core_back(q):
        return spread(15, q, own_half, half, core_mate)

    def core_arrival(q):
        return spread(15, q, half - own_half, half, core_mate)

    def at_stage(t, offset, condition, action):
        q = t - offset
        live = jnp.logical_and(q >= 0, q < chunks)
        if condition is not None:
            live = jnp.logical_and(live, condition)
        pl.when(live)(lambda: action(jnp.clip(q, 0, chunks - 1)))

    def b_rows(flow):
        return pl.ds(b_own[flow], piece)

    def a_forward(q):
        pl.when(is_mid)(lambda: c_a_mid(q).start())
        pl.when(jnp.logical_not(is_mid))(lambda: c_a_in(q).start())

    def begin(q):
        c_core(q).wait()
        core_in[q] = core_in[q] + held[place(q, own_half, half)]
        c_y(q).start()
        for flow in range(2):
            if roots[flow] > 0:
                pl.when(line == 0)(lambda flow=flow: c_b_up(q, flow).start())
            if roots[flow] < last:
                pl.when(line == last)(lambda flow=flow: c_b_down(q, flow).start())

    def after_y(q):
        c_y(q).wait_recv()
        y_in[q] = y_in[q] + core_in[q, rows_at(a_own, piece), :]
        pl.when(depth == 0)(lambda: a_forward(q))

    def a_reduce(q):
        c_a_in(q).wait_recv()
        y_in[q] = y_in[q] + a_in[q]
        a_forward(q)

    def a_total(q):
        c_a_mid(q).wait_recv()
        held[place(q, own_half + a_own, piece)] = y_in[q] + a_mid[q]
        pl.when(depth > 0)(lambda: c_a_out(q).start())
        c_y_back(q).start()

    def a_back(q):
        c_a_out(q).wait_recv()
        pl.when(depth > 0)(lambda: c_a_out(q).start())
        c_y_back(q).start()

    def b_pass_up(q, flow):
        c_b_up(q, flow).wait_recv()
        core_in[q, b_rows(flow), :] = core_in[q, b_rows(flow), :] + b_low[flow, q]
        c_b_up(q, flow).start()

    def b_pass_down(q, flow):
        c_b_down(q, flow).wait_recv()
        core_in[q, b_rows(flow), :] = core_in[q, b_rows(flow), :] + b_high[flow, q]
        c_b_down(q, flow).start()

    def b_root(q, flow):
        if roots[flow] > 0:
            c_b_up(q, flow).wait_recv()
            core_in[q, b_rows(flow), :] = core_in[q, b_rows(flow), :] + b_low[flow, q]
        if roots[flow] < last:
            c_b_down(q, flow).wait_recv()
            core_in[q, b_rows(flow), :] = core_in[q, b_rows(flow), :] + b_high[flow, q]
        c_rung(q, flow).start()

    def b_total(q, flow):
        c_rung(q, flow).wait_recv()
        held[place(q, own_half + b_own[flow], piece)] = core_in[q, b_rows(flow), :] + rung[q]
        if roots[flow] > 0:
            c_b_out(q, flow, 0).start()
        if roots[flow] < last:
            c_b_out(q, flow, 1).start()

    def b_back(q, flow):
        c_b_out(q, flow, 0).wait_recv()
        pl.when(jnp.logical_and(line < roots[flow], has_down))(lambda: c_b_out(q, flow, 0).start())
        pl.when(jnp.logical_and(line > roots[flow], has_up))(lambda: c_b_out(q, flow, 1).start())

    def gather(q):
        y_back_arrival(q).wait_recv()
        c_core_back(q).start()

    def proj_rows(span):
        return pl.ds(pl.multiple_of(samples + span * deep, deep), deep)

    def c_proj(span, shift):
        cols = pl.ds(pl.multiple_of(mine_at * width, width), width)
        return pltpu.make_async_remote_copy(
            src_ref=held.at[pl.ds(pl.multiple_of(height + span * deep, deep), deep), cols],
            dst_ref=left_ref.at[proj_rows(span), :],
            send_sem=proj_send.at[shift, span],
            recv_sem=proj_sem.at[span],
            device_id=(row, lax.rem(col + shift, groups)),
            device_id_type=MESH,
        )

    is_owner = col == owner

    def finish(q):
        core_arrival(q).wait_recv()
        span, slice_of = span_and_slice(q)

        @pl.when(jnp.logical_and(is_owner, slice_of == mine_at))
        def _():
            for shift in range(1, groups):
                c_proj(span, shift).start()
            left_ref[proj_rows(span), :] = held[place(q, 0, deep)]

    slice_at = pl.multiple_of(mine_at * width, width)

    def fetched(span):
        rows = pl.ds(span * deep, deep)
        return samples_ref.at[rows, pl.ds(slice_at, width)], left_ref.at[rows, :]

    def fetch(shift, span):
        source, target = fetched(span)
        return pltpu.make_async_remote_copy(
            src_ref=source,
            dst_ref=target,
            send_sem=fetch_send.at[shift, span],
            recv_sem=fetch_sem.at[0, span],
            device_id=(row, lax.rem(col + shift, groups)),
            device_id_type=MESH,
        )

    def own(span):
        return pltpu.make_async_copy(*fetched(span), fetch_sem.at[1, span])

    @pl.when(is_owner)
    def _():
        for span in range(spans):
            for shift in range(1, groups):
                fetch(shift, span).start()
            own(span).start()

    def take(first, count):
        @pl.when(is_owner)
        def _():
            for span in range(first, first + count):
                own(span).wait()

        @pl.when(jnp.logical_not(is_owner))
        def _():
            for span in range(first, first + count):
                fetch(1, span).wait_recv()

        size = count * deep
        high, low = split(left_ref[pl.ds(first * deep, size), :])
        lefts[2 * first * deep : 2 * first * deep + size, :] = high
        lefts[2 * first * deep + size : 2 * (first * deep + size), :] = low

    def prepare_slice(span_at, fresh):
        if fresh:
            load(span_at).wait()
            pl.when(span_at + 2 < per_group)(lambda: load(span_at + 2).start())
        hit = jnp.logical_and(is_owner, span_at == mine_at)

        def put(k, b, omega):
            high, low = split(omega)
            rows, cols = pl.ds(k * block, block), pl.ds(b * block, block)
            rights[0, rows, cols] = high
            rights[1, rows, cols] = low

        def omega_at(k, b):
            cols = pl.ds(pl.multiple_of(span_at * width + b * block, block), block)
            mask_col = (col * columns + span_at * width) // block + b
            keep = mask_ref[row * height // block + k, mask_col].astype(jnp.float32)
            return held[k * block : (k + 1) * block, cols] * keep

        for b in range(width // block):
            for k in range(height // block):
                put(k, b, omega_at(k, b))

        @pl.when(hit)
        def _():
            for b in range(width // block):
                omega = omega_at(b, b)
                diag = diag_ref[:, b * block : (b + 1) * block]
                put(b, b, jnp.where(on_diagonal(0, 0, omega.shape), diag, omega))

    def project(span_at, first, count):
        size = count * deep
        base = 2 * first * deep
        both = dot(lefts[base : base + 2 * size, :], rights[0])
        total = both[:size, :] + both[size:, :] + dot(lefts[base : base + size, :], rights[1])
        cols = pl.ds(pl.multiple_of(span_at * width, width), width)
        held[height + first * deep : height + first * deep + size, cols] = total

    tile = sample_tiles.shape[2]
    steps = columns // tile
    most = samples - deep
    row_at = row * height

    def load_samples(u):
        cols = pl.ds(pl.multiple_of(u * tile, tile), tile)
        return pltpu.make_async_copy(
            samples_ref.at[pl.ds(0, deep), cols], sample_tiles.at[u % 2], sample_sem.at[u % 2]
        )

    def prepare():
        pl.when(jnp.logical_not(is_owner))(lambda: c_proj(0, 1).wait_recv())
        fill_lefts(early_lefts, left_ref, [(0, most), (samples, deep)])

    def step_early(u):
        cols = pl.ds(pl.multiple_of(u * tile, tile), tile)
        load_samples(u).wait()
        fill_rights(early_rights, 0, held[height : height + most, cols])
        fill_rights(early_rights, most, sample_tiles[u % 2])
        pl.when(u + 2 < steps)(lambda: load_samples(u + 2).start())
        col_at = col * columns + u * tile

        def update(hit):
            for begin_at in range(0, height, block):
                rows = pl.ds(begin_at, block)
                omega = masked(mask_ref, held[rows, cols], row_at + begin_at, col_at, block)
                if hit:
                    diag = diag_ref[:, pl.ds(pl.multiple_of(col_at - row_at, tile), tile)]
                    omega = jnp.where(on_diagonal(row_at + begin_at, col_at, omega.shape), diag, omega)
                held[rows, cols] = omega - cross_of(early_lefts, early_rights, rows)

        hit = crosses(row_at, col_at, (height, tile))
        pl.when(hit)(lambda: update(True))
        pl.when(jnp.logical_not(hit))(lambda: update(False))

    load_samples(0).start()
    load_samples(1).start()
    prepare_slice(0, True)
    take(0, 1)
    slack = SLACK
    near = NEAR

    depth_of_pipe = 2 * near + slack * (lines + 1)
    per_slice = width // tile
    early_at = per_group + max(inside, slack + 1) - 1 + depth_of_pipe

    @pl.loop(0, chunks + depth_of_pipe)
    def _(t):
        begin_t = t
        t = begin_t - near
        at_stage(t, near + slack * (lines + 1 - depth), None, finish)
        for flow in range(2):
            away = jnp.abs(line - roots[flow])
            at_stage(t, slack * (1 + middle + away), away > 0, lambda q, flow=flow: b_back(q, flow))
        at_stage(t, slack * (lines + 1 - depth), None, gather)
        if middle > 1:
            at_stage(t, slack * (lines - depth), jnp.logical_not(is_mid), a_back)
        for flow in range(2):
            at_stage(t, slack * (1 + middle), line == roots[flow], lambda q, flow=flow: b_total(q, flow))
        at_stage(t, slack * (1 + middle), is_mid, a_total)
        for flow in range(2):
            at_stage(t, slack * middle, line == roots[flow], lambda q, flow=flow: b_root(q, flow))
        if middle > 1:
            at_stage(t, slack * (1 + depth), depth > 0, a_reduce)
        for flow in range(2):
            root = roots[flow]
            if root > 1:
                at_stage(t, slack * line, jnp.logical_and(line > 0, line < root), lambda q, flow=flow: b_pass_up(q, flow))
            if root < last - 1:
                at_stage(t, slack * (last - line), jnp.logical_and(line > root, line < last), lambda q, flow=flow: b_pass_down(q, flow))
        at_stage(t, slack, None, after_y)
        t = begin_t
        pl.when(t < per_group)(lambda: project(t, 0, 1))
        pl.when(t == per_group)(lambda: take(1, spans - 1))
        again = t - per_group

        @pl.when(jnp.logical_and(jnp.logical_and(again >= 0, again < inside * per_group), again % inside == 0))
        def _():
            project(again // inside, 1, spans - 1)

        at_stage(t, 0, None, lambda q: c_core(q).start())
        at_stage(t, near, None, begin)
        pl.when(begin_t == early_at)(prepare)
        pl.when(begin_t + 1 < per_group)(lambda: prepare_slice(begin_t + 1, True))
        following = begin_t + 1 - per_group

        @pl.when(
            jnp.logical_and(
                jnp.logical_and(following >= 0, following < inside * per_group), following % inside == 0
            )
        )
        def _():
            prepare_slice(following // inside, False)

        now = begin_t - early_at
        at_slice, turn = now // inside, now % inside
        live = jnp.logical_and(jnp.logical_and(now >= 0, at_slice < per_group), turn < per_slice)
        pl.when(live)(lambda: step_early(at_slice * per_slice + turn))

    def all_sent(kind, ref):
        copy(kind, 0, ref, ref, core_mate).wait_send()

    all_sent(1, y_in)
    pl.when(is_mid)(lambda: all_sent(3, y_in))
    pl.when(jnp.logical_not(is_mid))(lambda: all_sent(2, y_in))
    pl.when(depth > 0)(lambda: all_sent(4, y_in))
    all_sent(5, y_in)
    for flow in range(2):
        root = roots[flow]
        pl.when(line < root)(lambda flow=flow: all_sent(6 + flow, y_in))
        pl.when(line > root)(lambda flow=flow: all_sent(8 + flow, y_in))
        pl.when(line == root)(lambda: all_sent(10, y_in))
        pl.when(jnp.logical_and(line <= root, has_down))(lambda flow=flow: all_sent(11 + 2 * flow, y_in))
        pl.when(jnp.logical_and(line >= root, has_up))(lambda flow=flow: all_sent(12 + 2 * flow, y_in))
    all_sent(15, core_in)

    @pl.when(is_owner)
    def _():
        for span in range(spans):
            for shift in range(1, groups):
                fetch(shift, span).wait_send()
        for span in range(spans):
            for shift in range(1, groups):
                c_proj(span, shift).wait_send()

    @pl.when(jnp.logical_not(is_owner))
    def _():
        for span in range(1, spans):
            c_proj(span, 1).wait_recv()


def per_device(samples, values, diag_entries, block_mask):
    height, order = values.shape
    count = samples.shape[0]
    groups = lax.axis_size("col")
    lines = lax.axis_size("row") // 4
    per_group = order // height
    block = groups * order // block_mask.shape[0]
    diag = diag_entries[None, :]
    anywhere = pl.BlockSpec(memory_space=pl.ANY)
    in_smem = pl.BlockSpec(memory_space=pltpu.SMEM)
    in_vmem = pl.BlockSpec(memory_space=VM)
    deep = min(64, count // 2)
    spans = count // deep
    chunks = spans * per_group
    piece = deep // 8
    kinds = 16
    tile = min(2 * block, height)
    flows = lambda *lead: VM((*lead, chunks, piece, height), jnp.float32)
    dma = pltpu.SemaphoreType.DMA
    left, held = pl.pallas_call(
        functools.partial(reduce_kernel, lines, groups, per_group),
        out_shape=(
            VM((2 * count, height), jnp.float32),
            VM((height + count, order), jnp.float32),
        ),
        in_specs=[anywhere, anywhere, in_vmem, in_smem],
        out_specs=(in_vmem, in_vmem),
        scratch_shapes=[
            VM((chunks, deep // 2, height), jnp.float32),
            flows(),
            flows(),
            flows(),
            flows(2),
            flows(2),
            flows(),
            dma((kinds,)),
            dma((chunks,)),
            dma((kinds, chunks)),
            VM((2 * count, height), jnp.bfloat16),
            VM((2, height, height), jnp.bfloat16),
            dma((per_group,)),
            dma((groups, spans)),
            dma((2, spans)),
            dma((groups, spans)),
            dma((spans,)),
            VM((height, 3 * count), jnp.bfloat16),
            VM((3 * count, tile), jnp.bfloat16),
            VM((2, deep, tile), jnp.float32),
            dma((2,)),
        ],
        compiler_params=pltpu.CompilerParams(
            collective_id=1, has_side_effects=True, vmem_limit_bytes=REDUCE_LIMIT
        ),
    )(samples, values, diag, block_mask)

    left, held = (pltpu.with_memory_space_constraint(x, VM) for x in (left, held))
    wide = min(4 * block, height)
    return pl.pallas_call(
        functools.partial(update_kernel, per_group, deep),
        out_shape=jax.ShapeDtypeStruct((height, order), jnp.float32),
        in_specs=[in_vmem, in_vmem, anywhere, in_vmem],
        out_specs=anywhere,
        scratch_shapes=[
            VM((height, 3 * count), jnp.bfloat16),
            VM((3 * count, wide), jnp.bfloat16),
            VM((2, count - deep, wide), jnp.float32),
            VM((2, height, wide), jnp.float32),
            dma((2,)),
            dma((2,)),
        ],
        compiler_params=pltpu.CompilerParams(vmem_limit_bytes=UPDATE_LIMIT),
    )(left, held, samples, diag)


def solution(mesh):
    in_specs = (P(None, "col"), P("row", "col"), P("row"), P())
    out_specs = P("row", "col")
    return jax.shard_map(
        per_device, mesh=mesh, in_specs=in_specs, out_specs=out_specs, check_vma=False
    )
```
